32 devices in a mesh: rep: 2 (over y), req: 4 (over z), mp: 4 (over x, core).
Axes of the slice: x: 2, y: 2, z: 4, core: 2. Of those that a mesh axis runs over, the one named last changes fastest.
Arguments:
- hidden_in: bfloat16 [128, 2, 8192], P(('rep', 'req'), None, 'mp'), parts along dimension 0, may hold values from -6 to 6
- frozen_query_rows: bfloat16 [128, 2, 8192], P(('rep', 'req'), None, 'mp'), parts along dimension 0, may hold values from -6 to 86
- new_kv: bfloat16 [128, 2, 2, 1024], P(('rep', 'req'), None, None, 'mp'), parts along dimension 0, may hold values from -6 to 31
- adapter_of: int32 [128], P(('rep', 'req')), parts along dimension 0, may hold values from 0 to 7, as said below
- adapter_home: int32 [16], P('rep'), parts along dimension 0, may hold values from 0 to 7, as said below
- a_store: bfloat16 [16, 64, 8192], P(('rep', 'req'), None, 'mp'), parts along dimension 0, may hold values from -0.0625 to 0.0625
- b_store: bfloat16 [16, 64, 8192], P(('rep', 'req'), None, 'mp'), parts along dimension 0, may hold values from -0.75 to 0.75
- kv_pool: bfloat16 [2, 1024, 16, 1024], P(None, ('rep', 'req'), None, 'mp'), parts along dimension 1, may hold values from -6 to 31
- page_table: int32 [128, 8], P(('rep', 'req')), parts along dimension 0, may hold values from 0 to 127, as said below
- cached_len: int32 [128], P(('rep', 'req')), parts along dimension 0, may hold values from 32 to 128
- new_group: int32 [128], P(('rep', 'req')), parts along dimension 0, may hold values from 0 to 3, as said below
Outputs:
- attended: bfloat16 [128, 2, 8192], P(('rep', 'req'), None, 'mp'), parts along dimension 0
- cache: bfloat16 [2, 128, 128, 1024], P(None, ('rep', 'req'), None, 'mp'), parts along dimension 1
The draws below stay inside these ranges and needn't reach their ends.
There are 2 independent parts, one for each index of `rep`. The reference program is written for one: setup_inputs(seed, part) draws one part's arguments, and reference() takes and returns one part's arrays. A program takes and returns all parts, laid end to end along the dimension named above; each array names one. Nothing has to cross between parts.
Inputs may be any that keep to these rules, and one draw needn't show every extreme that they name: A permutation: adapter a lives in store slot adapter_home[a], which belongs to group adapter_home[a] div 2. `adapter_of`: the requests of one group (new rows h * 16 to h * 16 + 15) use adapters of min(16, number of groups) different owners, at most 4 requests an owner, a number reached in every group; all requests of one group whose adapters have one owner use the same adapter. `page_table`: the rows of one group name each of its 128 pages once. `new_group`: A request keeps its slot (row mod 16); the same 4 slots keep their group in every group; every group receives exactly one request into each slot; no group sends more than 3 requests to one other group, and some pair of groups reaches it.
All inputs are finite; a program needn't handle non-finite values.
Results may differ from the reference program's by a relative error of at most 0.0069.
Values may be sent and summed in bfloat16 or wider, within the bound.
A program may use at most 64 MiB of HBM per device.

```python
import jax
import jax.numpy as jnp
from jax import lax

D = 8192
HEAD = 128
RANK = 64
STEPS = 2
PAGE = 16
REQ_DEV = 16
CTX = 128
ADAPT_DEV = 2
QW = 8192
KVW = 1024
REQUESTS = 64
ADAPTERS = 8
PAGES_REQ = 8
POOL_DEV = 128
POOL = 512


def shared_home(key):
    return jax.random.permutation(jax.random.fold_in(key, 17), ADAPTERS).astype(jnp.int32)


def draw_adapter_home(key, part):
    return shared_home(key)


def draw_adapter_of(key, part):
    owner_count = ADAPTERS // ADAPT_DEV
    group_count = REQUESTS // REQ_DEV
    home_slots = shared_home(key)
    inverse = jnp.argsort(home_slots, stable=True).astype(jnp.int32)
    order_keys = jax.random.split(jax.random.fold_in(key, 23), group_count)
    owner_order = jax.vmap(lambda subkey: jax.random.permutation(subkey, owner_count))(order_keys)
    slot_keys = jax.random.split(jax.random.fold_in(key, 29), group_count)
    slot_order = jax.vmap(lambda subkey: jax.random.permutation(subkey, REQ_DEV))(slot_keys)
    owners = jnp.take_along_axis(owner_order, slot_order % owner_count, axis=1)
    local_pick = jax.random.randint(jax.random.fold_in(key, 31), (group_count, owner_count), 0, ADAPT_DEV)
    chosen = jnp.take_along_axis(local_pick, owners, axis=1)
    return inverse[(owners * ADAPT_DEV + chosen).reshape(-1)].astype(jnp.int32)


def draw_new_group(key, part):
    group_count = REQUESTS // REQ_DEV
    stay_count = REQ_DEV // 4
    spread = jax.random.permutation(jax.random.fold_in(key, 37), group_count)
    target = jax.random.permutation(jax.random.fold_in(key, 41), group_count)
    slot_rank = jax.random.permutation(jax.random.fold_in(key, 43), REQ_DEV)
    group_ids = jnp.arange(group_count)[:, None]
    moved = target[(spread[group_ids] + slot_rank[None, :]) % group_count]
    return jnp.where(slot_rank[None, :] < stay_count, group_ids, moved).reshape(-1).astype(jnp.int32)


def draw_page_table(key, part):
    group_count = REQUESTS // REQ_DEV
    page_keys = jax.random.split(jax.random.fold_in(key, 47), group_count)
    perms = jax.vmap(lambda subkey: jax.random.permutation(subkey, POOL_DEV))(page_keys)
    return perms.reshape(REQUESTS, PAGES_REQ).astype(jnp.int32)


def draw_cached_len(key, part):
    lengths = jax.random.randint(jax.random.fold_in(key, 53), (REQUESTS,), CTX // 4, CTX + 1)
    return lengths.at[0].set(CTX).at[1].set(CTX // 4).astype(jnp.int32)


def draw_frozen_query_rows(key, part):
    q_shape = (REQUESTS, STEPS, QW)
    return jnp.clip(jax.random.normal(jax.random.fold_in(key, 1), q_shape), -6.0, 6.0).astype(jnp.bfloat16)


def draw_kv_pool(key, part):
    pool_shape = (2, POOL, PAGE, KVW)
    return jnp.clip(jax.random.normal(jax.random.fold_in(key, 4), pool_shape), -6.0, 6.0).astype(jnp.bfloat16)


def draw_new_kv(key, part):
    kv_shape = (REQUESTS, STEPS, 2, KVW)
    return jnp.clip(jax.random.normal(jax.random.fold_in(key, 8), kv_shape), -6.0, 6.0).astype(jnp.bfloat16)


def level_of(key, extent, cuts, least, high):
    loudness = 1.0
    for position, blocks in cuts:
        steps = jax.random.uniform(jax.random.fold_in(jax.random.fold_in(key, 6), position), (blocks,), jnp.float32, least / len(cuts), high / len(cuts))
        loudness = loudness * jnp.repeat(jnp.exp(steps), extent[position] // blocks).reshape((-1,) + (1,) * (len(extent) - 1 - position))
    return loudness


def normal_values(key, shape, scale, bound, shards=(), held_as=jnp.bfloat16):
    factor_of = level_of(key, shape, shards, -0.22, 0.18) if shards else 1.0
    result = jax.random.normal(key, shape, jnp.float32) * scale * factor_of
    return jnp.minimum(jnp.maximum(result, -bound), bound).astype(held_as)


def setup_inputs(seed: int = 0, part: int = 0) -> dict:
    arg_keys = jax.random.split(jax.random.key(seed), 12)
    part_splits = jax.random.split(jax.random.fold_in(arg_keys[11], part), 12)
    return {
        "hidden_in": normal_values(part_splits[0], (REQUESTS, STEPS, D), 1.0, 6.0, ((0, 4), (2, 4))),
        "frozen_query_rows": draw_frozen_query_rows(jax.random.fold_in(jax.random.fold_in(arg_keys[11], part), 71), part),
        "new_kv": draw_new_kv(jax.random.fold_in(jax.random.fold_in(arg_keys[11], part), 71), part),
        "adapter_of": draw_adapter_of(jax.random.fold_in(jax.random.fold_in(arg_keys[11], part), 71), part),
        "adapter_home": draw_adapter_home(jax.random.fold_in(jax.random.fold_in(arg_keys[11], part), 71), part),
        "a_store": normal_values(part_splits[5], (ADAPTERS, RANK, D), D ** -0.5, 0.0625, ((0, 4), (2, 4))),
        "b_store": normal_values(part_splits[6], (ADAPTERS, RANK, QW), RANK ** -0.5, 0.75, ((0, 4), (2, 4))),
        "kv_pool": draw_kv_pool(jax.random.fold_in(jax.random.fold_in(arg_keys[11], part), 71), part),
        "page_table": draw_page_table(jax.random.fold_in(jax.random.fold_in(arg_keys[11], part), 71), part),
        "cached_len": draw_cached_len(jax.random.fold_in(jax.random.fold_in(arg_keys[11], part), 71), part),
        "new_group": draw_new_group(jax.random.fold_in(jax.random.fold_in(arg_keys[11], part), 71), part),
    }


NEG_FILL = -1.0e30


def attend(query_vectors, cached_keys, cached_values, length, fresh_kv):
    row_count, step_count, q_width = query_vectors.shape
    context = cached_keys.shape[1]
    kv_width = cached_keys.shape[2]
    kv_heads = kv_width // HEAD
    per_kv = q_width // kv_width
    score_scale = HEAD ** -0.5
    q_split = query_vectors.reshape(row_count, step_count, kv_heads, per_kv, HEAD)
    k_split = cached_keys.reshape(row_count, context, kv_heads, HEAD)
    v_split = cached_values.reshape(row_count, context, kv_heads, HEAD)
    new_keys = fresh_kv[:, :, 0].reshape(row_count, step_count, kv_heads, HEAD)
    new_values = fresh_kv[:, :, 1].reshape(row_count, step_count, kv_heads, HEAD)
    old_scores = jnp.einsum("bskgd,bjkd->bskgj", q_split, k_split, preferred_element_type=jnp.float32) * score_scale
    visible = jnp.arange(context)[None, :] < length[:, None]
    old_scores = jnp.where(visible[:, None, None, None, :], old_scores, NEG_FILL)
    new_scores = jnp.einsum("bskgd,btkd->bskgt", q_split, new_keys, preferred_element_type=jnp.float32) * score_scale
    causal = jnp.arange(step_count)[None, :] <= jnp.arange(step_count)[:, None]
    new_scores = jnp.where(causal[None, :, None, None, :], new_scores, NEG_FILL)
    scores = jnp.concatenate([old_scores, new_scores], axis=-1)
    row_max = jnp.max(scores, axis=-1, keepdims=True)
    weights = jnp.exp(scores - row_max)
    probabilities = (weights / jnp.sum(weights, axis=-1, keepdims=True)).astype(jnp.bfloat16)
    attention_out = jnp.einsum("bskgj,bjkd->bskgd", probabilities[..., :context], v_split, preferred_element_type=jnp.float32)
    attention_out = attention_out + jnp.einsum("bskgt,btkd->bskgd", probabilities[..., context:], new_values, preferred_element_type=jnp.float32)
    return attention_out.reshape(row_count, step_count, q_width).astype(jnp.bfloat16)


def reference(hidden_in, frozen_query_rows, new_kv, adapter_of, adapter_home, a_store, b_store, kv_pool, page_table, cached_len, new_group):
    old_rows = jnp.arange(REQUESTS, dtype=jnp.int32)
    new_rows = (new_group * REQ_DEV + old_rows % REQ_DEV).astype(jnp.int32)
    source = jnp.zeros((REQUESTS,), jnp.int32).at[new_rows].set(old_rows)

    def per_request(fresh_position_row):
        old_row = source[fresh_position_row]
        store_slot = adapter_home[adapter_of[fresh_position_row]]
        panel_a = a_store[store_slot]
        up_projection_panel = b_store[store_slot]
        complete_rank_product = jnp.dot(hidden_in[fresh_position_row], panel_a.T, preferred_element_type=jnp.float32).astype(jnp.bfloat16)
        adapter_query_delta = jnp.dot(complete_rank_product, up_projection_panel, preferred_element_type=jnp.float32)
        query_vectors = (frozen_query_rows[fresh_position_row].astype(jnp.float32) + adapter_query_delta).astype(jnp.bfloat16)
        page_ids = ((old_row // REQ_DEV) * POOL_DEV + page_table[old_row]).astype(jnp.int32)
        kv_pages = jnp.take(kv_pool, page_ids, axis=1).reshape(2, CTX, KVW)
        attended_row = attend(query_vectors[None], kv_pages[0][None], kv_pages[1][None], cached_len[old_row][None], new_kv[fresh_position_row][None])[0]
        return attended_row, kv_pages

    attended, cache_rows = lax.map(per_request, old_rows)
    cache = jnp.transpose(cache_rows, (1, 0, 2, 3))
    return (attended, cache)
```

```python
import functools

import jax
import jax.numpy as jnp
from jax import lax
from jax.experimental import pallas as pl
from jax.experimental.pallas import tpu as pltpu
from jax.sharding import PartitionSpec as P

HEAD = 128
NEG_FILL = -1e30
MESH = pl.DeviceIdType.MESH
VMEM = pltpu.VMEM
SMEM = pltpu.SMEM
HBM = pltpu.HBM


def attention(work, steps, qr):
    f32, bf16 = jnp.float32, jnp.bfloat16
    scale = HEAD ** (-0.5)
    context = work[0][1].shape[0]
    position = lax.broadcasted_iota(jnp.int32, (qr, context), 1)
    scores, extra = [], []
    for q, keys, _, length, fresh in work:
        s = lax.dot_general(q, keys, (((1,), (1,)), ((), ())), preferred_element_type=f32)
        scores.append(jnp.where(position < length, s * scale, NEG_FILL))
        qf = q.astype(f32)
        extra.append([jnp.sum(qf * fresh[t][0], axis=1, keepdims=True) for t in range(steps)])
    scores = jnp.concatenate(scores, axis=0)
    step_of = lax.rem(lax.broadcasted_iota(jnp.int32, (len(work) * qr, 1), 0), steps)
    extra = [
        jnp.where(
            step_of >= t, jnp.concatenate([e[t] for e in extra], axis=0) * scale, NEG_FILL
        )
        for t in range(steps)
    ]
    top = jnp.max(scores, axis=1, keepdims=True)
    for e in extra:
        top = jnp.maximum(top, e)
    weights = jnp.exp(scores - top)
    extra = [jnp.exp(e - top) for e in extra]
    norm = jnp.sum(weights, axis=1, keepdims=True)
    for e in extra:
        norm = norm + e
    prob = (weights / norm).astype(bf16)
    extra = [(e / norm).astype(bf16).astype(f32) for e in extra]
    out = []
    for n, (_, _, values, _, fresh) in enumerate(work):
        part = slice(n * qr, (n + 1) * qr)
        o = jnp.dot(prob[part], values, preferred_element_type=f32)
        for t in range(steps):
            o = o + extra[t][part] * fresh[t][1]
        out.append(o.astype(bf16))
    return out


def exchange(
    cfg,
    given,
    outs,
    held,
    in_sem,
    h_send,
    h_all,
    r_part,
    r_all,
    d_send,
    d_all,
    q_rows,
    wide,
    meta_send,
    meta_all,
    meta_s,
    page_send,
    h_ss,
    h_rs,
    r_ss,
    r_rs,
    d_ss,
    d_rs,
    m_ss,
    m_rs,
    p_ss,
    p_rs,
    l_sem,
):
    groups, mps, per_group, steps, block, store_count, rank, pages, page, move_cap = cfg
    rows, att, info, q_last, fresh_last, len_last = outs
    f32, bf16 = jnp.float32, jnp.bfloat16
    rep = lax.axis_index("rep")
    me = lax.axis_index("req")
    mp = lax.axis_index("mp")
    fetch = [
        pltpu.make_async_copy(src, dst, in_sem.at[i])
        for i, (src, dst) in enumerate(zip(given, held))
    ]
    for f in fetch:
        f.start()
    (
        adapter_of,
        adapter_home,
        page_table,
        cached_len,
        new_group,
        hidden,
        pool,
        frozen,
        a_panels,
        b_panels,
        fresh,
    ) = held
    width = hidden.shape[2]
    lanes = store_count * rank
    kv_width = pool.shape[3]
    kv_heads = kv_width // HEAD
    per_kv = width // kv_width
    sent_rows = groups * block
    own_rows = per_group * steps
    qr = per_kv * steps

    def peer(d):
        return lax.rem(me + d, groups)

    def send_to(d):
        return (rep, peer(d), mp)

    barrier = pltpu.get_barrier_semaphore()
    for d in range(1, groups):
        pl.semaphore_signal(barrier, inc=1, device_id=send_to(d), device_id_type=MESH)
    for d in range(1, mps):
        pl.semaphore_signal(
            barrier, inc=1, device_id=(rep, me, lax.rem(mp + d, mps)), device_id_type=MESH
        )

    for f in fetch[:6]:
        f.wait()

    owners, picks, targets = [], [], []
    for r in range(per_group):
        home = adapter_home[adapter_of[r]]
        owner = home // store_count
        picks.append(home - owner * store_count)
        place = jnp.int32(0)
        for o in owners:
            place = place + (o == owner).astype(jnp.int32)
        owners.append(owner)
        targets.append(owner * block + place * steps)
    col = lax.broadcasted_iota(jnp.int32, (sent_rows, own_rows), 1)
    row = lax.broadcasted_iota(jnp.int32, (sent_rows, own_rows), 0)
    want = jnp.zeros((sent_rows, own_rows), jnp.int32)
    for r in range(per_group):
        want = jnp.where(col // steps == r, targets[r] + lax.rem(col, steps), want)
    pick_by_owner = (row == want).astype(f32).astype(bf16)

    def flat(ref):
        for r in range(per_group):
            wide[r * steps : (r + 1) * steps] = ref[r].astype(f32)
        return wide[...]

    h_out = jnp.dot(pick_by_owner, flat(hidden).astype(bf16), preferred_element_type=f32)
    h_send[...] = h_out.reshape(groups, block, width).astype(bf16)

    pl.semaphore_wait(barrier, groups - 1 + mps - 1)

    def copies(src, dst, ss, rs):
        out = {}
        for d in range(1, groups):
            out[d] = pltpu.make_async_remote_copy(
                src_ref=src(d),
                dst_ref=dst,
                send_sem=ss.at[d - 1],
                recv_sem=rs.at[d - 1],
                device_id=send_to(d),
                device_id_type=MESH,
            )
        return out

    h_cp = copies(lambda d: h_send.at[peer(d)], h_all.at[me], h_ss, h_rs)
    order = sorted(range(1, groups), key=lambda d: -min(d, groups - d))
    for d in order:
        h_cp[d].start()
    h_all[me] = h_send[me]

    lane = lax.broadcasted_iota(jnp.int32, (1, 128), 1)
    meta = jnp.zeros((1, 128), jnp.int32)
    for r in range(per_group):
        meta = jnp.where(lane == r, new_group[r], meta)
        meta = jnp.where(lane == per_group + r, cached_len[r], meta)
        meta = jnp.where(lane == 2 * per_group + owners[r], picks[r], meta)
    meta_send[...] = meta
    m_cp = copies(lambda d: meta_send, meta_all.at[me], m_ss, m_rs)
    for d in order:
        m_cp[d].start()
    meta_all[me] = meta

    fetch[6].wait()
    p_cp, sources = {}, {}
    for d in order:
        dest = peer(d)
        count = jnp.int32(0)
        picked = [jnp.int32(0)] * move_cap
        for r in range(per_group):
            hit = new_group[r] == dest
            for k in range(move_cap):
                picked[k] = jnp.where(hit & (count == k), r, picked[k])
            count = count + hit.astype(jnp.int32)
        sources[d] = picked

    def pack_pages(k):
        for d in order:
            slot = (d - 1) * move_cap + k
            for j in range(pages):
                page_id = page_table[j, sources[d][k]]
                page_send[slot, :, pl.ds(j * page, page), :] = pool[:, page_id]
            p_cp[slot] = pltpu.make_async_remote_copy(
                src_ref=page_send.at[slot],
                dst_ref=rows.at[per_group + slot],
                send_sem=p_ss.at[slot],
                recv_sem=p_rs.at[slot],
                device_id=send_to(d),
                device_id_type=MESH,
            )
            if k == 0 or (k == 1 and d == order[0]):
                p_cp[slot].start()

    def send_pages(k):
        for d in order[1:] if k == 1 else order:
            p_cp[(d - 1) * move_cap + k].start()

    pack_pages(0)

    fetch[8].wait()
    for d in range(1, groups):
        h_cp[d].wait_recv()
    h_in = h_all[...].astype(f32).reshape(sent_rows, width).astype(bf16)
    r_part[...] = lax.dot_general(
        h_in, a_panels[...], (((1,), (1,)), ((), ())), preferred_element_type=f32
    )
    r_cp = {}
    for d in range(1, mps):
        r_cp[d] = pltpu.make_async_remote_copy(
            src_ref=r_part,
            dst_ref=r_all.at[mp],
            send_sem=r_ss.at[d - 1],
            recv_sem=r_rs.at[d - 1],
            device_id=(rep, me, lax.rem(mp + d, mps)),
            device_id_type=MESH,
        )
        r_cp[d].start()
    r_all[mp] = r_part[...]

    for d in range(1, groups):
        m_cp[d].wait_recv()
    local = pltpu.make_async_copy(meta_all, meta_s, l_sem)
    local.start()

    for k in range(1, move_cap):
        pack_pages(k)

    local.wait()
    mrow = lax.broadcasted_iota(jnp.int32, (sent_rows, lanes), 0) // block
    mlane = lax.broadcasted_iota(jnp.int32, (sent_rows, lanes), 1) // rank
    wanted = jnp.zeros((sent_rows, lanes), jnp.int32)
    for g in range(groups):
        wanted = jnp.where(mrow == g, meta_s[g, 0, 2 * per_group + me], wanted)

    fetch[9].wait()
    for d in range(1, mps):
        r_cp[d].wait_recv()
    total = r_all[0]
    for j in range(1, mps):
        total = total + r_all[j]
    total = jnp.where(mlane == wanted, total, 0.0).astype(bf16)
    delta = jnp.dot(total, b_panels[...], preferred_element_type=f32)
    d_send[...] = delta.reshape(groups, block, width).astype(bf16)
    d_cp = copies(lambda d: d_send.at[peer(d)], d_all.at[me], d_ss, d_rs)
    for d in order:
        d_cp[d].start()
    for k in range(1, move_cap):
        send_pages(k)
    d_all[me] = d_send[me]

    @pl.loop(0, per_group)
    def _(r):
        for j in range(pages):
            rows[r, :, pl.ds(j * page, page), :] = pool[:, page_table[j, r]]

    fetch[7].wait()
    fetch[10].wait()
    entry_slot = [jnp.int32(r) for r in range(per_group)]
    entry_len = [cached_len[r] for r in range(per_group)]
    source = [jnp.int32(r) for r in range(per_group)]
    for d in range(1, groups):
        origin = lax.rem(me + groups - d, groups)
        count = jnp.int32(0)
        slots = [jnp.int32(0)] * move_cap
        for r in range(per_group):
            hit = meta_s[origin, 0, r] == me
            for k in range(move_cap):
                slots[k] = jnp.where(hit & (count == k), r, slots[k])
            source[r] = jnp.where(
                hit,
                per_group + (d - 1) * move_cap + jnp.minimum(count, move_cap - 1),
                source[r],
            )
            count = count + hit.astype(jnp.int32)
        for k in range(move_cap):
            entry_slot.append(slots[k])
            entry_len.append(meta_s[origin, 0, per_group + slots[k]])
    told = jnp.zeros((1, 128), jnp.int32)
    for r in range(per_group):
        told = jnp.where(lane == r, source[r], told)
    info[...] = told

    own_row = lax.broadcasted_iota(jnp.int32, (own_rows, sent_rows), 0)
    own_col = lax.broadcasted_iota(jnp.int32, (own_rows, sent_rows), 1)
    back = jnp.zeros((own_rows, sent_rows), jnp.int32)
    for r in range(per_group):
        back = jnp.where(own_row // steps == r, targets[r] + lax.rem(own_row, steps), back)
    back = (own_col == back).astype(f32).astype(bf16)
    ri = lax.broadcasted_iota(jnp.int32, (per_group * qr, per_kv * own_rows), 0)
    ci = lax.broadcasted_iota(jnp.int32, (per_group * qr, per_kv * own_rows), 1)
    place = (
        ci == (lax.rem(ri, qr) // steps) * own_rows + (ri // qr) * steps + lax.rem(ri, steps)
    )
    place = place.astype(f32).astype(bf16)
    base_rows = flat(frozen)

    for d in range(1, groups):
        d_cp[d].wait_recv()
    d_in = d_all[...].astype(f32).reshape(sent_rows, width).astype(bf16)
    queries = base_rows + jnp.dot(back, d_in, preferred_element_type=f32)
    for h in range(kv_heads):
        stack = jnp.concatenate(
            [
                queries[:, (h * per_kv + i) * HEAD : (h * per_kv + i + 1) * HEAD]
                for i in range(per_kv)
            ],
            axis=0,
        ).astype(bf16)
        got = jnp.dot(place, stack, preferred_element_type=f32)
        q_rows[:, h] = got.reshape(per_group, qr, HEAD).astype(bf16)

    def attend(items):
        work, places = [], []
        for entry, slot, length in items:
            new = [fresh[slot, t].astype(f32) for t in range(steps)]
            for h in range(kv_heads):
                cols = slice(h * HEAD, (h + 1) * HEAD)
                work.append(
                    (
                        q_rows[slot, h],
                        rows[entry, 0, :, cols],
                        rows[entry, 1, :, cols],
                        length,
                        [(n[0:1, cols], n[1:2, cols]) for n in new],
                    )
                )
                places.append((entry, h))
        for (entry, h), o in zip(places, attention(work, steps, qr)):
            att[entry, h] = o

    near = sorted(range(1, groups), key=lambda d: min(d, groups - d))
    for n, d in enumerate(near):
        e = per_group + (d - 1) * move_cap + move_cap - 1
        for t in range(steps):
            fresh_last[n, 2 * t : 2 * t + 2] = fresh[entry_slot[e], t].astype(f32)
        q_last[n] = q_rows[entry_slot[e]]
        len_last[n] = jnp.zeros((1, 128), jnp.int32) + entry_len[e]
    for r in range(0, per_group, 4):
        attend([(e, e, entry_len[e]) for e in range(r, min(r + 4, per_group))])
    for k in range(move_cap - 1):
        for n in range(0, len(near), 3):
            items = []
            for d in near[n : n + 3]:
                p_cp[(d - 1) * move_cap + k].wait_recv()
                e = per_group + (d - 1) * move_cap + k
                items.append((e, entry_slot[e], entry_len[e]))
            attend(items)

    for d in range(1, groups):
        h_cp[d].wait_send()
        m_cp[d].wait_send()
        d_cp[d].wait_send()
    for d in range(1, mps):
        r_cp[d].wait_send()
    for slot in p_cp:
        p_cp[slot].wait_send()
    for d in near:
        p_cp[(d - 1) * move_cap + move_cap - 1].wait_recv()


def finish(cfg, rows, att, info, q_last, fresh_last, len_last, att_out, cache_out, info_s, late, i_sem, c_sem):
    groups, mps, per_group, steps, block, store_count, rank, pages, page, move_cap = cfg
    f32, bf16 = jnp.float32, jnp.bfloat16
    _, kv_heads, qr, _ = att.shape
    per_kv = qr // steps
    own_rows = per_group * steps
    told = pltpu.make_async_copy(info, info_s, i_sem)
    told.start()
    told.wait()
    source = [info_s[0, r] for r in range(per_group)]
    out = [
        pltpu.make_async_copy(rows.at[source[r]], cache_out.at[:, r], c_sem.at[r])
        for r in range(per_group)
    ]
    for c in out:
        c.start()
    late[...] = att[...]
    near = sorted(range(1, groups), key=lambda d: min(d, groups - d))
    for n in range(0, len(near), 3):
        work, places = [], []
        for i, d in list(enumerate(near))[n : n + 3]:
            entry = per_group + (d - 1) * move_cap + move_cap - 1
            new = fresh_last[i]
            for h in range(kv_heads):
                cols = slice(h * HEAD, (h + 1) * HEAD)
                work.append(
                    (
                        q_last[i, h],
                        rows[entry, 0, :, cols],
                        rows[entry, 1, :, cols],
                        len_last[i],
                        [
                            (new[2 * t : 2 * t + 1, cols], new[2 * t + 1 : 2 * t + 2, cols])
                            for t in range(steps)
                        ],
                    )
                )
                places.append((entry, h))
        for (entry, h), o in zip(places, attention(work, steps, qr)):
            late[entry, h] = o
    pr = lax.broadcasted_iota(jnp.int32, (per_kv * own_rows, per_group * qr), 0)
    pc = lax.broadcasted_iota(jnp.int32, (per_kv * own_rows, per_group * qr), 1)
    in_row = lax.rem(pr, own_rows)
    spread = (
        pc == (in_row // steps) * qr + (pr // own_rows) * steps + lax.rem(in_row, steps)
    )
    spread = spread.astype(f32).astype(bf16)
    for h in range(kv_heads):
        stack = jnp.concatenate([late[source[r], h] for r in range(per_group)], axis=0)
        got = jnp.dot(spread, stack, preferred_element_type=f32)
        for i in range(per_kv):
            for r in range(per_group):
                at = i * own_rows + r * steps
                att_out[r, :, (h * per_kv + i) * HEAD : (h * per_kv + i + 1) * HEAD] = got[
                    at : at + steps
                ].astype(bf16)
    for c in out:
        c.wait()


def per_device(
    hidden_in,
    frozen_query_rows,
    new_kv,
    adapter_of,
    adapter_home,
    a_store,
    b_store,
    kv_pool,
    page_table,
    cached_len,
    new_group,
):
    groups = lax.axis_size("req")
    mps = lax.axis_size("mp")
    per_group, steps, width = hidden_in.shape
    store_count, rank, _ = a_store.shape
    pages, page = page_table.shape[1], kv_pool.shape[2]
    kv_width = kv_pool.shape[3]
    context = pages * page
    move_cap = -(-(per_group - per_group // 4) // groups)
    cap = -(-per_group // min(16, groups))
    block = -(-cap * steps // 8) * 8
    lanes = store_count * rank
    qr = width // kv_width * steps
    kv_heads = kv_width // HEAD
    moved = (groups - 1) * move_cap
    last = groups - 1
    entries = per_group + moved
    bf16, f32, i32 = jnp.bfloat16, jnp.float32, jnp.int32
    cfg = (groups, mps, per_group, steps, block, store_count, rank, pages, page, move_cap)
    dma = pltpu.SemaphoreType.DMA
    given = (
        adapter_of,
        adapter_home,
        page_table.T,
        cached_len,
        new_group,
        hidden_in,
        kv_pool,
        frozen_query_rows,
        a_store.reshape(lanes, width),
        b_store.reshape(lanes, width),
        new_kv,
    )
    passed = (
        jax.ShapeDtypeStruct((entries, 2, context, kv_width), bf16),
        jax.ShapeDtypeStruct((entries, kv_heads, qr, HEAD), bf16),
        jax.ShapeDtypeStruct((1, 128), i32),
        jax.ShapeDtypeStruct((last, kv_heads, qr, HEAD), bf16),
        jax.ShapeDtypeStruct((last, 2 * steps, kv_width), f32),
        jax.ShapeDtypeStruct((last, 1, 128), i32),
    )
    scratch = [
        VMEM((groups, block, width), bf16),
        VMEM((groups, block, width), bf16),
        VMEM((groups * block, lanes), f32),
        VMEM((mps, groups * block, lanes), f32),
        VMEM((groups, block, width), bf16),
        VMEM((groups, block, width), bf16),
        VMEM((per_group, kv_heads, qr, HEAD), bf16),
        VMEM((per_group * steps, width), f32),
        VMEM((1, 128), i32),
        VMEM((groups, 1, 128), i32),
        SMEM((groups, 1, 128), i32),
        VMEM((moved, 2, context, kv_width), bf16),
        dma((groups - 1,)),
        dma((groups - 1,)),
        dma((mps - 1,)),
        dma((mps - 1,)),
        dma((groups - 1,)),
        dma((groups - 1,)),
        dma((groups - 1,)),
        dma((groups - 1,)),
        dma((moved,)),
        dma((moved,)),
        dma,
    ]

    def first(*refs):
        n = len(given)
        held = n + len(passed)
        exchange(
            cfg, refs[:n], refs[n:held], refs[held : held + n], refs[held + n], *refs[held + n + 1 :]
        )

    between = pl.pallas_call(
        first,
        out_shape=passed,
        in_specs=[pl.BlockSpec(memory_space=HBM)] * len(given),
        out_specs=[pl.BlockSpec(memory_space=VMEM)] * len(passed),
        scratch_shapes=[SMEM(g.shape, g.dtype) for g in given[:5]]
        + [VMEM(g.shape, g.dtype) for g in given[5:]]
        + [dma((len(given),))]
        + scratch,
        compiler_params=pltpu.CompilerParams(
            collective_id=0, has_side_effects=True, vmem_limit_bytes=32 * 2**20
        ),
        name="exchange",
    )(*[pltpu.with_memory_space_constraint(g, HBM) for g in given])
    return pl.pallas_call(
        functools.partial(finish, cfg),
        out_shape=(
            jax.ShapeDtypeStruct((per_group, steps, width), bf16),
            jax.ShapeDtypeStruct((2, per_group, context, kv_width), bf16),
        ),
        in_specs=[pl.BlockSpec(memory_space=VMEM)] * len(passed),
        out_specs=(pl.BlockSpec(memory_space=VMEM), pl.BlockSpec(memory_space=HBM)),
        scratch_shapes=[
            SMEM((1, 128), i32),
            VMEM((entries, kv_heads, qr, HEAD), bf16),
            dma,
            dma((per_group,)),
        ],
        compiler_params=pltpu.CompilerParams(vmem_limit_bytes=16 * 2**20),
        name="finish",
    )(*between)


def solution(mesh):
    placed = (
        P(("rep", "req"), None, "mp"),
        P(("rep", "req"), None, "mp"),
        P(("rep", "req"), None, None, "mp"),
        P(("rep", "req")),
        P("rep"),
        P(("rep", "req"), None, "mp"),
        P(("rep", "req"), None, "mp"),
        P(None, ("rep", "req"), None, "mp"),
        P(("rep", "req"), None),
        P(("rep", "req")),
        P(("rep", "req")),
    )
    return jax.shard_map(
        per_device,
        mesh=mesh,
        in_specs=placed,
        out_specs=(P(("rep", "req"), None, "mp"), P(None, ("rep", "req"), None, "mp")),
        check_vma=False,
    )
```

```python
import functools

import jax
import jax.numpy as jnp
from jax import lax
from jax.experimental import pallas as pl
from jax.experimental.pallas import tpu as pltpu
from jax.sharding import PartitionSpec as P

HEAD = 128
NEG_FILL = -1e30
MESH = pl.DeviceIdType.MESH
VMEM = pltpu.VMEM
SMEM = pltpu.SMEM
HBM = pltpu.HBM


def probabilities(work, steps, qr):
    f32, bf16 = jnp.float32, jnp.bfloat16
    scale = HEAD ** (-0.5)
    context = work[0][1].shape[0]
    position = lax.broadcasted_iota(jnp.int32, (qr, context), 1)
    scores, extra = [], []
    for q, keys, length, fresh in work:
        s = lax.dot_general(q, keys, (((1,), (1,)), ((), ())), preferred_element_type=f32)
        scores.append(jnp.where(position < length, s * scale, NEG_FILL))
        qf = q.astype(f32)
        extra.append([jnp.sum(qf * fresh[t][0], axis=1, keepdims=True) for t in range(steps)])
    scores = jnp.concatenate(scores, axis=0)
    step_of = lax.rem(lax.broadcasted_iota(jnp.int32, (len(work) * qr, 1), 0), steps)
    extra = [
        jnp.where(
            step_of >= t, jnp.concatenate([e[t] for e in extra], axis=0) * scale, NEG_FILL
        )
        for t in range(steps)
    ]
    top = jnp.max(scores, axis=1, keepdims=True)
    for e in extra:
        top = jnp.maximum(top, e)
    weights = jnp.exp(scores - top)
    extra = [jnp.exp(e - top) for e in extra]
    norm = jnp.sum(weights, axis=1, keepdims=True)
    for e in extra:
        norm = norm + e
    prob = (weights / norm).astype(bf16)
    extra = [(e / norm).astype(bf16).astype(f32) for e in extra]
    added = []
    for n, (_, _, _, fresh) in enumerate(work):
        part = slice(n * qr, (n + 1) * qr)
        o = extra[0][part] * fresh[0][1]
        for t in range(1, steps):
            o = o + extra[t][part] * fresh[t][1]
        added.append(o)
    return prob, added


def exchange(
    cfg,
    given,
    outs,
    held,
    in_sem,
    h_send,
    h_all,
    r_part,
    r_all,
    d_send,
    d_all,
    q_rows,
    wide,
    meta_send,
    meta_all,
    meta_s,
    page_send,
    att,
    h_ss,
    h_rs,
    r_ss,
    r_rs,
    d_ss,
    d_rs,
    m_ss,
    m_rs,
    p_ss,
    p_rs,
    l_sem,
):
    groups, mps, per_group, steps, block, store_count, rank, pages, page, move_cap = cfg
    rows, early, info, prob_last, new_last = outs
    f32, bf16 = jnp.float32, jnp.bfloat16
    rep = lax.axis_index("rep")
    me = lax.axis_index("req")
    mp = lax.axis_index("mp")
    fetch = [
        pltpu.make_async_copy(src, dst, in_sem.at[i])
        for i, (src, dst) in enumerate(zip(given, held))
    ]
    for f in fetch:
        f.start()
    (
        adapter_of,
        adapter_home,
        page_table,
        cached_len,
        new_group,
        hidden,
        pool,
        frozen,
        a_panels,
        b_panels,
        fresh,
    ) = held
    width = hidden.shape[2]
    lanes = store_count * rank
    kv_width = pool.shape[3]
    kv_heads = kv_width // HEAD
    per_kv = width // kv_width
    sent_rows = groups * block
    own_rows = per_group * steps
    qr = per_kv * steps

    upper = me // (groups // 2)

    def target(j):
        down = groups - 1 - j
        down = down - jnp.clip(me - down + 1, 0, 1)
        up = j + jnp.clip(j - me + 1, 0, 1)
        return down + upper * (up - down)

    def step_to(j):
        return lax.rem(target(j) - me + groups, groups)

    def send_to(j):
        return (rep, target(j), mp)

    barrier = pltpu.get_barrier_semaphore()
    for j in range(groups - 1):
        pl.semaphore_signal(barrier, inc=1, device_id=send_to(j), device_id_type=MESH)
    for d in range(1, mps):
        pl.semaphore_signal(
            barrier, inc=1, device_id=(rep, me, lax.rem(mp + d, mps)), device_id_type=MESH
        )

    for f in fetch[:6]:
        f.wait()

    owners, picks, targets = [], [], []
    for r in range(per_group):
        home = adapter_home[adapter_of[r]]
        owner = home // store_count
        picks.append(home - owner * store_count)
        place = jnp.int32(0)
        for o in owners:
            place = place + (o == owner).astype(jnp.int32)
        owners.append(owner)
        targets.append(owner * block + place * steps)
    col = lax.broadcasted_iota(jnp.int32, (sent_rows, own_rows), 1)
    row = lax.broadcasted_iota(jnp.int32, (sent_rows, own_rows), 0)
    want = jnp.zeros((sent_rows, own_rows), jnp.int32)
    for r in range(per_group):
        want = jnp.where(col // steps == r, targets[r] + lax.rem(col, steps), want)
    pick_by_owner = (row == want).astype(f32).astype(bf16)

    def flat(ref):
        for r in range(per_group):
            wide[r * steps : (r + 1) * steps] = ref[r].astype(f32)
        return wide[...]

    h_out = jnp.dot(pick_by_owner, flat(hidden).astype(bf16), preferred_element_type=f32)
    h_send[...] = h_out.reshape(groups, block, width).astype(bf16)

    pl.semaphore_wait(barrier, groups - 1 + mps - 1)

    def copies(src, dst, ss, rs):
        out = []
        for j in range(groups - 1):
            d = step_to(j)
            out.append(
                pltpu.make_async_remote_copy(
                    src_ref=src(target(j)),
                    dst_ref=dst,
                    send_sem=ss.at[d - 1],
                    recv_sem=rs.at[d - 1],
                    device_id=send_to(j),
                    device_id_type=MESH,
                )
            )
        return out

    h_cp = copies(lambda t: h_send.at[t], h_all.at[me], h_ss, h_rs)
    for c in h_cp:
        c.start()
    h_all[me] = h_send[me]

    lane = lax.broadcasted_iota(jnp.int32, (1, 128), 1)
    meta = jnp.zeros((1, 128), jnp.int32)
    for r in range(per_group):
        meta = jnp.where(lane == r, new_group[r], meta)
        meta = jnp.where(lane == per_group + r, cached_len[r], meta)
        meta = jnp.where(lane == 2 * per_group + owners[r], picks[r], meta)
    meta_send[...] = meta
    m_cp = copies(lambda t: meta_send, meta_all.at[me], m_ss, m_rs)
    for c in m_cp:
        c.start()
    meta_all[me] = meta

    fetch[6].wait()
    sources = []
    for j in range(groups - 1):
        dest = target(j)
        count = jnp.int32(0)
        picked = [jnp.int32(0)] * move_cap
        for r in range(per_group):
            hit = new_group[r] == dest
            for k in range(move_cap):
                picked[k] = jnp.where(hit & (count == k), r, picked[k])
            count = count + hit.astype(jnp.int32)
        sources.append(picked)

    p_cp = {}

    def pack_pages(k):
        for j in range(groups - 1):
            slot = (step_to(j) - 1) * move_cap + k
            for i in range(pages):
                page_id = page_table[i, sources[j][k]]
                page_send[slot, :, pl.ds(i * page, page), :] = pool[:, page_id]
            for half in range(2):
                at = slice(None) if k < move_cap - 1 else half
                p_cp[j, k, half] = pltpu.make_async_remote_copy(
                    src_ref=page_send.at[slot, at],
                    dst_ref=rows.at[per_group + slot, at],
                    send_sem=p_ss.at[slot, half],
                    recv_sem=p_rs.at[slot, half],
                    device_id=send_to(j),
                    device_id_type=MESH,
                )
                if k < move_cap - 1:
                    break

    others = range(groups - 1)
    queue = [(j, 0) for j in others] + [(0, k) for k in range(1, move_cap)]
    queue += [(j, k) for k in range(1, move_cap) for j in others[:0:-1]]
    ahead = groups if move_cap > 1 else groups // 2

    def send_pages(some):
        for j, k in some:
            for half in range(1 if k < move_cap - 1 else 2):
                p_cp[j, k, half].start()

    pack_pages(0)
    send_pages([s for s in queue[:ahead] if s[1] == 0])

    fetch[8].wait()
    for c in h_cp:
        c.wait_recv()
    h_in = h_all[...].astype(f32).reshape(sent_rows, width).astype(bf16)
    r_part[...] = lax.dot_general(
        h_in, a_panels[...], (((1,), (1,)), ((), ())), preferred_element_type=f32
    )
    r_cp = {}
    for d in range(1, mps):
        r_cp[d] = pltpu.make_async_remote_copy(
            src_ref=r_part,
            dst_ref=r_all.at[mp],
            send_sem=r_ss.at[d - 1],
            recv_sem=r_rs.at[d - 1],
            device_id=(rep, me, lax.rem(mp + d, mps)),
            device_id_type=MESH,
        )
        r_cp[d].start()
    r_all[mp] = r_part[...]

    for c in m_cp:
        c.wait_recv()
    local = pltpu.make_async_copy(meta_all, meta_s, l_sem)
    local.start()

    for k in range(1, move_cap):
        pack_pages(k)
    send_pages([s for s in queue[:ahead] if s[1] > 0])

    local.wait()
    mrow = lax.broadcasted_iota(jnp.int32, (sent_rows, lanes), 0) // block
    mlane = lax.broadcasted_iota(jnp.int32, (sent_rows, lanes), 1) // rank
    wanted = jnp.zeros((sent_rows, lanes), jnp.int32)
    for g in range(groups):
        wanted = jnp.where(mrow == g, meta_s[g, 0, 2 * per_group + me], wanted)

    fetch[9].wait()
    for d in range(1, mps):
        r_cp[d].wait_recv()
    total = r_all[0]
    for j in range(1, mps):
        total = total + r_all[j]
    total = jnp.where(mlane == wanted, total, 0.0).astype(bf16)
    delta = jnp.dot(total, b_panels[...], preferred_element_type=f32)
    d_send[...] = delta.reshape(groups, block, width).astype(bf16)
    d_cp = copies(lambda t: d_send.at[t], d_all.at[me], d_ss, d_rs)
    for c in d_cp:
        c.start()
    send_pages(queue[ahead:])
    d_all[me] = d_send[me]

    @pl.loop(0, per_group)
    def _(r):
        for j in range(pages):
            rows[r, :, pl.ds(j * page, page), :] = pool[:, page_table[j, r]]

    fetch[7].wait()
    fetch[10].wait()
    entry_slot = [jnp.int32(r) for r in range(per_group)]
    entry_len = [cached_len[r] for r in range(per_group)]
    source = [jnp.int32(r) for r in range(per_group)]
    for d in range(1, groups):
        origin = lax.rem(me + groups - d, groups)
        count = jnp.int32(0)
        slots = [jnp.int32(0)] * move_cap
        for r in range(per_group):
            hit = meta_s[origin, 0, r] == me
            for k in range(move_cap):
                slots[k] = jnp.where(hit & (count == k), r, slots[k])
            source[r] = jnp.where(
                hit,
                per_group + (d - 1) * move_cap + jnp.minimum(count, move_cap - 1),
                source[r],
            )
            count = count + hit.astype(jnp.int32)
        for k in range(move_cap):
            entry_slot.append(slots[k])
            entry_len.append(meta_s[origin, 0, per_group + slots[k]])
    near = sorted(range(1, groups), key=lambda d: min(d, groups - d))
    late = [per_group + (d - 1) * move_cap + move_cap - 1 for d in near]
    told_row = lax.broadcasted_iota(jnp.int32, info.shape, 0)
    told_lane = lax.broadcasted_iota(jnp.int32, info.shape, 1)
    told = jnp.zeros(info.shape, jnp.int32)
    for r in range(per_group):
        told = jnp.where(told_row == r, source[r], told)
    for n, e in enumerate(late):
        counts = [(source[r] == e).astype(jnp.int32) for r in range(per_group)]
        real = functools.reduce(jnp.maximum, counts)
        told = jnp.where(
            told_row == per_group + n, jnp.where(told_lane == 1, real, entry_slot[e]), told
        )
    info[...] = told

    own_row = lax.broadcasted_iota(jnp.int32, (own_rows, sent_rows), 0)
    own_col = lax.broadcasted_iota(jnp.int32, (own_rows, sent_rows), 1)
    back = jnp.zeros((own_rows, sent_rows), jnp.int32)
    for r in range(per_group):
        back = jnp.where(own_row // steps == r, targets[r] + lax.rem(own_row, steps), back)
    back = (own_col == back).astype(f32).astype(bf16)
    ri = lax.broadcasted_iota(jnp.int32, (per_group * qr, per_kv * own_rows), 0)
    ci = lax.broadcasted_iota(jnp.int32, (per_group * qr, per_kv * own_rows), 1)
    place = (
        ci == (lax.rem(ri, qr) // steps) * own_rows + (ri // qr) * steps + lax.rem(ri, steps)
    )
    place = place.astype(f32).astype(bf16)
    base_rows = flat(frozen)

    for c in d_cp:
        c.wait_recv()
    d_in = d_all[...].astype(f32).reshape(sent_rows, width).astype(bf16)
    queries = base_rows + jnp.dot(back, d_in, preferred_element_type=f32)
    for h in range(kv_heads):
        stack = jnp.concatenate(
            [
                queries[:, (h * per_kv + i) * HEAD : (h * per_kv + i + 1) * HEAD]
                for i in range(per_kv)
            ],
            axis=0,
        ).astype(bf16)
        got = jnp.dot(place, stack, preferred_element_type=f32)
        q_rows[:, h] = got.reshape(per_group, qr, HEAD).astype(bf16)

    def cols(h):
        return slice(h * HEAD, (h + 1) * HEAD)

    def scored(items):
        work = []
        for entry, slot, length in items:
            new = [fresh[slot, t].astype(f32) for t in range(steps)]
            for h in range(kv_heads):
                pairs = [(n[0:1, cols(h)], n[1:2, cols(h)]) for n in new]
                work.append((q_rows[slot, h], rows[entry, 0, :, cols(h)], length, pairs))
        return probabilities(work, steps, qr)

    def arrived(slot, at, half):
        pltpu.make_async_remote_copy(
            src_ref=page_send.at[slot, at],
            dst_ref=rows.at[per_group + slot, at],
            send_sem=p_ss.at[slot, half],
            recv_sem=p_rs.at[slot, half],
            device_id=send_to(0),
            device_id_type=MESH,
        ).wait_recv()

    def attend(items):
        prob, added = scored(items)
        for n, (entry, h) in enumerate((i[0], h) for i in items for h in range(kv_heads)):
            part = prob[n * qr : (n + 1) * qr]
            o = jnp.dot(part, rows[entry, 1, :, cols(h)], preferred_element_type=f32)
            att[entry, h] = (o + added[n]).astype(bf16)

    for r in range(0, per_group, 4):
        attend([(e, e, entry_len[e]) for e in range(r, min(r + 4, per_group))])
    for k in range(move_cap - 1):
        for n in range(0, len(near), 3):
            items = []
            for d in near[n : n + 3]:
                slot = (d - 1) * move_cap + k
                arrived(slot, slice(None), 0)
                e = per_group + slot
                items.append((e, entry_slot[e], entry_len[e]))
            attend(items)
    for e in late:
        att[e] = jnp.zeros(att.shape[1:], bf16)
    pr = lax.broadcasted_iota(jnp.int32, (per_kv * own_rows, per_group * qr), 0)
    pc = lax.broadcasted_iota(jnp.int32, (per_kv * own_rows, per_group * qr), 1)
    in_row = lax.rem(pr, own_rows)
    spread = (
        pc == (in_row // steps) * qr + (pr // own_rows) * steps + lax.rem(in_row, steps)
    )
    spread = spread.astype(f32).astype(bf16)
    for h in range(kv_heads):
        stack = jnp.concatenate([att[source[r], h] for r in range(per_group)], axis=0)
        got = jnp.dot(spread, stack, preferred_element_type=f32)
        for i in range(per_kv):
            wide[:, (h * per_kv + i) * HEAD : (h * per_kv + i + 1) * HEAD] = got[
                i * own_rows : (i + 1) * own_rows
            ]
    for r in range(per_group):
        early[r] = wide[r * steps : (r + 1) * steps].astype(bf16)

    for n in range(0, len(near), 3):
        batch = late[n : n + 3]
        for e in batch:
            arrived(e - per_group, 0, 0)
        prob, added = scored([(e, entry_slot[e], entry_len[e]) for e in batch])
        for i, (j, h) in enumerate((j, h) for j in range(len(batch)) for h in range(kv_heads)):
            prob_last[n + j, h] = prob[i * qr : (i + 1) * qr]
            new_last[n + j, h] = added[i]

    for c in h_cp + m_cp + d_cp:
        c.wait_send()
    for d in range(1, mps):
        r_cp[d].wait_send()
    for p in p_cp.values():
        p.wait_send()
    for e in late:
        arrived(e - per_group, 1, 1)


def finish(cfg, rows, early, info, prob_last, new_last, att_out, cache_out, late, c_sem, e_sem):
    groups, mps, per_group, steps, block, store_count, rank, pages, page, move_cap = cfg
    f32, bf16 = jnp.float32, jnp.bfloat16
    last, kv_heads, qr, _ = new_last.shape
    per_kv = qr // steps
    told = info[...]
    source = [told[r, 0] for r in range(per_group)]
    out = [
        pltpu.make_async_copy(rows.at[source[r]], cache_out.at[:, r], c_sem.at[r])
        for r in range(per_group)
    ]
    for c in out:
        c.start()
    for r in range(per_group):
        from_last = (source[r] >= per_group) & (
            lax.rem(source[r] - per_group, move_cap) == move_cap - 1
        )

        @pl.when(jnp.logical_not(from_last))
        def _():
            pltpu.make_async_copy(early.at[r], att_out.at[r], e_sem.at[r]).start()

    near = sorted(range(1, groups), key=lambda d: min(d, groups - d))
    entry = [per_group + (d - 1) * move_cap + move_cap - 1 for d in near]
    for n in range(last):
        for h in range(kv_heads):
            values = rows[entry[n], 1, :, h * HEAD : (h + 1) * HEAD]
            o = new_last[n, h] + jnp.dot(prob_last[n, h], values, preferred_element_type=f32)
            for i in range(per_kv):
                late[n, :, (h * per_kv + i) * HEAD : (h * per_kv + i + 1) * HEAD] = o[
                    i * steps : (i + 1) * steps
                ].astype(bf16)
    for n in range(last):
        slot = told[per_group + n, 0]

        @pl.when(told[per_group + n, 1] == 1)
        def _():
            pltpu.make_async_copy(late.at[n], att_out.at[slot], e_sem.at[slot]).start()

    for r in range(per_group):
        out.append(pltpu.make_async_copy(early.at[r], att_out.at[r], e_sem.at[r]))
    for c in out:
        c.wait()


def per_device(
    hidden_in,
    frozen_query_rows,
    new_kv,
    adapter_of,
    adapter_home,
    a_store,
    b_store,
    kv_pool,
    page_table,
    cached_len,
    new_group,
):
    groups = lax.axis_size("req")
    mps = lax.axis_size("mp")
    per_group, steps, width = hidden_in.shape
    store_count, rank, _ = a_store.shape
    pages, page = page_table.shape[1], kv_pool.shape[2]
    kv_width = kv_pool.shape[3]
    context = pages * page
    move_cap = -(-(per_group - per_group // 4) // groups)
    cap = -(-per_group // min(16, groups))
    block = -(-cap * steps // 8) * 8
    lanes = store_count * rank
    qr = width // kv_width * steps
    kv_heads = kv_width // HEAD
    moved = (groups - 1) * move_cap
    last = groups - 1
    entries = per_group + moved
    bf16, f32, i32 = jnp.bfloat16, jnp.float32, jnp.int32
    cfg = (groups, mps, per_group, steps, block, store_count, rank, pages, page, move_cap)
    dma = pltpu.SemaphoreType.DMA
    given = (
        adapter_of,
        adapter_home,
        page_table.T,
        cached_len,
        new_group,
        hidden_in,
        kv_pool,
        frozen_query_rows,
        a_store.reshape(lanes, width),
        b_store.reshape(lanes, width),
        new_kv,
    )
    passed = (
        jax.ShapeDtypeStruct((entries, 2, context, kv_width), bf16),
        jax.ShapeDtypeStruct((per_group, steps, width), bf16),
        jax.ShapeDtypeStruct((-(-(per_group + last) // 8) * 8, 128), i32),
        jax.ShapeDtypeStruct((last, kv_heads, qr, context), bf16),
        jax.ShapeDtypeStruct((last, kv_heads, qr, HEAD), f32),
    )
    scratch = [
        VMEM((groups, block, width), bf16),
        VMEM((groups, block, width), bf16),
        VMEM((groups * block, lanes), f32),
        VMEM((mps, groups * block, lanes), f32),
        VMEM((groups, block, width), bf16),
        VMEM((groups, block, width), bf16),
        VMEM((per_group, kv_heads, qr, HEAD), bf16),
        VMEM((per_group * steps, width), f32),
        VMEM((1, 128), i32),
        VMEM((groups, 1, 128), i32),
        SMEM((groups, 1, 128), i32),
        VMEM((moved, 2, context, kv_width), bf16),
        VMEM((entries, kv_heads, qr, HEAD), bf16),
        dma((groups - 1,)),
        dma((groups - 1,)),
        dma((mps - 1,)),
        dma((mps - 1,)),
        dma((groups - 1,)),
        dma((groups - 1,)),
        dma((groups - 1,)),
        dma((groups - 1,)),
        dma((moved, 2)),
        dma((moved, 2)),
        dma,
    ]

    def first(*refs):
        n = len(given)
        held = n + len(passed)
        exchange(
            cfg, refs[:n], refs[n:held], refs[held : held + n], refs[held + n], *refs[held + n + 1 :]
        )

    between = pl.pallas_call(
        first,
        out_shape=passed,
        in_specs=[pl.BlockSpec(memory_space=HBM)] * len(given),
        out_specs=[pl.BlockSpec(memory_space=VMEM)] * len(passed),
        scratch_shapes=[SMEM(g.shape, g.dtype) for g in given[:5]]
        + [VMEM(g.shape, g.dtype) for g in given[5:]]
        + [dma((len(given),))]
        + scratch,
        compiler_params=pltpu.CompilerParams(
            collective_id=0, has_side_effects=True, vmem_limit_bytes=32 * 2**20
        ),
        name="exchange",
    )(*[pltpu.with_memory_space_constraint(g, HBM) for g in given])
    return pl.pallas_call(
        functools.partial(finish, cfg),
        out_shape=(
            jax.ShapeDtypeStruct((per_group, steps, width), bf16),
            jax.ShapeDtypeStruct((2, per_group, context, kv_width), bf16),
        ),
        in_specs=[
            pl.BlockSpec(memory_space=m) for m in (VMEM, VMEM, VMEM, VMEM, VMEM)
        ],
        out_specs=[pl.BlockSpec(memory_space=HBM)] * 2,
        scratch_shapes=[
            VMEM((last, steps, width), bf16),
            dma((per_group,)),
            dma((per_group,)),
        ],
        compiler_params=pltpu.CompilerParams(vmem_limit_bytes=16 * 2**20),
        name="finish",
    )(*between)


def solution(mesh):
    placed = (
        P(("rep", "req"), None, "mp"),
        P(("rep", "req"), None, "mp"),
        P(("rep", "req"), None, None, "mp"),
        P(("rep", "req")),
        P("rep"),
        P(("rep", "req"), None, "mp"),
        P(("rep", "req"), None, "mp"),
        P(None, ("rep", "req"), None, "mp"),
        P(("rep", "req"), None),
        P(("rep", "req")),
        P(("rep", "req")),
    )
    return jax.shard_map(
        per_device,
        mesh=mesh,
        in_specs=placed,
        out_specs=(P(("rep", "req"), None, "mp"), P(None, ("rep", "req"), None, "mp")),
        check_vma=False,
    )
```

```python
import functools

import jax
import jax.numpy as jnp
from jax import lax
from jax.experimental import pallas as pl
from jax.experimental.pallas import tpu as pltpu
from jax.sharding import PartitionSpec as P

HEAD = 128
NEG_FILL = -1e30
MESH = pl.DeviceIdType.MESH
VMEM = pltpu.VMEM
SMEM = pltpu.SMEM
HBM = pltpu.HBM


def probabilities(work, steps, qr):
    f32, bf16 = jnp.float32, jnp.bfloat16
    scale = HEAD ** (-0.5)
    context = work[0][1].shape[0]
    position = lax.broadcasted_iota(jnp.int32, (qr, context), 1)
    scores, extra = [], []
    for q, keys, length, fresh in work:
        s = lax.dot_general(q, keys, (((1,), (1,)), ((), ())), preferred_element_type=f32)
        scores.append(jnp.where(position < length, s * scale, NEG_FILL))
        qf = q.astype(f32)
        extra.append([jnp.sum(qf * fresh[t][0], axis=1, keepdims=True) for t in range(steps)])
    scores = jnp.concatenate(scores, axis=0)
    step_of = lax.rem(lax.broadcasted_iota(jnp.int32, (len(work) * qr, 1), 0), steps)
    extra = [
        jnp.where(
            step_of >= t, jnp.concatenate([e[t] for e in extra], axis=0) * scale, NEG_FILL
        )
        for t in range(steps)
    ]
    top = jnp.max(scores, axis=1, keepdims=True)
    for e in extra:
        top = jnp.maximum(top, e)
    weights = jnp.exp(scores - top)
    extra = [jnp.exp(e - top) for e in extra]
    norm = jnp.sum(weights, axis=1, keepdims=True)
    for e in extra:
        norm = norm + e
    prob = (weights / norm).astype(bf16)
    extra = [(e / norm).astype(bf16).astype(f32) for e in extra]
    added = []
    for n, (_, _, _, fresh) in enumerate(work):
        part = slice(n * qr, (n + 1) * qr)
        o = extra[0][part] * fresh[0][1]
        for t in range(1, steps):
            o = o + extra[t][part] * fresh[t][1]
        added.append(o)
    return prob, added


def exchange(
    cfg,
    given,
    outs,
    held,
    in_sem,
    h_send,
    h_all,
    r_part,
    r_all,
    d_send,
    d_all,
    q_rows,
    wide,
    meta_send,
    meta_all,
    meta_s,
    page_send,
    att,
    h_ss,
    h_rs,
    r_ss,
    r_rs,
    d_ss,
    d_rs,
    m_ss,
    m_rs,
    p_ss,
    p_rs,
    l_sem,
    here,
    columns,
    everyone,
):
    groups, mps, per_group, steps, block, store_count, rank, pages, page, move_cap = cfg
    rows, early, info, prob_last, new_last = outs
    f32, bf16 = jnp.float32, jnp.bfloat16
    rep = lax.axis_index("rep")
    me = lax.axis_index("req")
    mp = lax.axis_index("mp")
    fetch = [
        pltpu.make_async_copy(src, dst, in_sem.at[i])
        for i, (src, dst) in enumerate(zip(given, held))
    ]
    for f in fetch:
        f.start()
    (
        adapter_of,
        adapter_home,
        page_table,
        cached_len,
        new_group,
        hidden,
        pool,
        frozen,
        a_panels,
        b_panels,
        fresh,
    ) = held
    width = hidden.shape[2]
    lanes = store_count * rank
    kv_width = pool.shape[3]
    kv_heads = kv_width // HEAD
    per_kv = width // kv_width
    sent_rows = groups * block
    own_rows = per_group * steps
    qr = per_kv * steps

    upper = me // (groups // 2)

    def target(j):
        down = groups - 1 - j
        down = down - jnp.clip(me - down + 1, 0, 1)
        up = j + jnp.clip(j - me + 1, 0, 1)
        return down + upper * (up - down)

    def step_to(j):
        return lax.rem(target(j) - me + groups, groups)

    def send_to(j):
        return (rep, target(j), mp)

    barrier = pltpu.get_barrier_semaphore()
    beside = [(rep, me, lax.rem(mp + d, mps)) for d in range(1, mps)]
    for t in range(1, groups):

        @pl.when(me < t)
        def _():
            pl.semaphore_signal(barrier, inc=1, device_id=(rep, t, mp), device_id_type=MESH)

    @pl.when(me == 0)
    def _():
        for device in beside:
            pl.semaphore_signal(barrier, inc=1, device_id=device, device_id_type=MESH)

    @pl.when(me > 0)
    def _():
        pl.semaphore_wait(barrier, me)

    for t in range(groups - 1):

        @pl.when(me > t)
        def _():
            pl.semaphore_signal(
                here.at[me], inc=1, device_id=(rep, t, mp), device_id_type=MESH
            )

    for f in fetch[:6]:
        f.wait()

    owners, picks, targets = [], [], []
    for r in range(per_group):
        home = adapter_home[adapter_of[r]]
        owner = home // store_count
        picks.append(home - owner * store_count)
        place = jnp.int32(0)
        for o in owners:
            place = place + (o == owner).astype(jnp.int32)
        owners.append(owner)
        targets.append(owner * block + place * steps)
    col = lax.broadcasted_iota(jnp.int32, (sent_rows, own_rows), 1)
    row = lax.broadcasted_iota(jnp.int32, (sent_rows, own_rows), 0)
    want = jnp.zeros((sent_rows, own_rows), jnp.int32)
    for r in range(per_group):
        want = jnp.where(col // steps == r, targets[r] + lax.rem(col, steps), want)
    pick_by_owner = (row == want).astype(f32).astype(bf16)

    def flat(ref):
        for r in range(per_group):
            wide[r * steps : (r + 1) * steps] = ref[r].astype(f32)
        return wide[...]

    h_out = jnp.dot(pick_by_owner, flat(hidden).astype(bf16), preferred_element_type=f32)
    h_send[...] = h_out.reshape(groups, block, width).astype(bf16)

    def copies(src, dst, ss, rs):
        out = []
        for j in range(groups - 1):
            d = step_to(j)
            out.append(
                pltpu.make_async_remote_copy(
                    src_ref=src(target(j)),
                    dst_ref=dst,
                    send_sem=ss.at[d - 1],
                    recv_sem=rs.at[d - 1],
                    device_id=send_to(j),
                    device_id_type=MESH,
                )
            )
        return out

    h_cp = copies(lambda t: h_send.at[t], h_all.at[me], h_ss, h_rs)

    for t in range(1, groups - 1):

        @pl.when(me < t)
        def _():
            pl.semaphore_wait(here.at[t], 1)

    @pl.when(upper == 0)
    def _():
        for c in h_cp[1:]:
            c.start()

    @pl.when(upper == 1)
    def _():
        for c in h_cp[:-1]:
            c.start()

    h_all[me] = h_send[me]

    lane = lax.broadcasted_iota(jnp.int32, (1, 128), 1)
    meta = jnp.zeros((1, 128), jnp.int32)
    for r in range(per_group):
        meta = jnp.where(lane == r, new_group[r], meta)
        meta = jnp.where(lane == per_group + r, cached_len[r], meta)
        meta = jnp.where(lane == 2 * per_group + owners[r], picks[r], meta)
    meta_send[...] = meta
    m_cp = copies(lambda t: meta_send, meta_all.at[me], m_ss, m_rs)
    meta_all[me] = meta

    fetch[6].wait()
    sources = []
    for j in range(groups - 1):
        dest = target(j)
        count = jnp.int32(0)
        picked = [jnp.int32(0)] * move_cap
        for r in range(per_group):
            hit = new_group[r] == dest
            for k in range(move_cap):
                picked[k] = jnp.where(hit & (count == k), r, picked[k])
            count = count + hit.astype(jnp.int32)
        sources.append(picked)

    p_cp = {}

    def pack_pages(k, peers):
        for j in peers:
            slot = (step_to(j) - 1) * move_cap + k
            for i in range(pages):
                page_id = page_table[i, sources[j][k]]
                page_send[slot, :, pl.ds(i * page, page), :] = pool[:, page_id]
            for half in range(2):
                at = slice(None) if k < move_cap - 1 else half
                p_cp[j, k, half] = pltpu.make_async_remote_copy(
                    src_ref=page_send.at[slot, at],
                    dst_ref=rows.at[per_group + slot, at],
                    send_sem=p_ss.at[slot, half],
                    recv_sem=p_rs.at[slot, half],
                    device_id=send_to(j),
                    device_id_type=MESH,
                )
                if k < move_cap - 1:
                    break

    others = range(groups - 1)
    queue = [(j, 0) for j in others] + [(0, k) for k in range(1, move_cap)]
    queue += [(j, k) for k in range(1, move_cap) for j in others[:0:-1]]
    ahead = groups if move_cap > 1 else groups // 2

    def send_pages(some):
        for j, k in some:
            for half in range(1 if k < move_cap - 1 else 2):
                p_cp[j, k, half].start()

    first = [s for s in queue[:ahead] if s[1] == 0]
    straight = groups // 2 - 1
    pack_pages(0, [straight])
    send_pages([s for s in first if s[0] == straight])

    @pl.when(me < groups - 1)
    def _():
        pl.semaphore_wait(here.at[groups - 1], 1)

    @pl.when(upper == 0)
    def _():
        h_cp[0].start()

    @pl.when(upper == 1)
    def _():
        h_cp[-1].start()

    for c in m_cp:
        c.start()
    pack_pages(0, [j for j in others if j != straight])
    send_pages([s for s in first if s[0] != straight])

    @pl.when(me == 0)
    def _():
        pl.semaphore_wait(barrier, mps - 1)
        for device in beside:
            pl.semaphore_signal(columns, inc=1, device_id=device, device_id_type=MESH)
        pl.semaphore_wait(columns, mps - 1)
        for t in range(1, groups):
            pl.semaphore_signal(everyone, inc=1, device_id=(rep, t, mp), device_id_type=MESH)

    @pl.when(me > 0)
    def _():
        pl.semaphore_wait(everyone, 1)

    fetch[8].wait()
    for c in h_cp:
        c.wait_recv()
    h_in = h_all[...].astype(f32).reshape(sent_rows, width).astype(bf16)
    r_part[...] = lax.dot_general(
        h_in, a_panels[...], (((1,), (1,)), ((), ())), preferred_element_type=f32
    )
    r_cp = {}
    for d in range(1, mps):
        r_cp[d] = pltpu.make_async_remote_copy(
            src_ref=r_part,
            dst_ref=r_all.at[mp],
            send_sem=r_ss.at[d - 1],
            recv_sem=r_rs.at[d - 1],
            device_id=(rep, me, lax.rem(mp + d, mps)),
            device_id_type=MESH,
        )
        r_cp[d].start()
    r_all[mp] = r_part[...]

    for c in m_cp:
        c.wait_recv()
    local = pltpu.make_async_copy(meta_all, meta_s, l_sem)
    local.start()

    for k in range(1, move_cap):
        pack_pages(k, others)
    send_pages([s for s in queue[:ahead] if s[1] > 0])

    local.wait()
    mrow = lax.broadcasted_iota(jnp.int32, (sent_rows, lanes), 0) // block
    mlane = lax.broadcasted_iota(jnp.int32, (sent_rows, lanes), 1) // rank
    wanted = jnp.zeros((sent_rows, lanes), jnp.int32)
    for g in range(groups):
        wanted = jnp.where(mrow == g, meta_s[g, 0, 2 * per_group + me], wanted)

    fetch[9].wait()
    for d in range(1, mps):
        r_cp[d].wait_recv()
    total = r_all[0]
    for j in range(1, mps):
        total = total + r_all[j]
    total = jnp.where(mlane == wanted, total, 0.0).astype(bf16)
    delta = jnp.dot(total, b_panels[...], preferred_element_type=f32)
    d_send[...] = delta.reshape(groups, block, width).astype(bf16)
    d_cp = copies(lambda t: d_send.at[t], d_all.at[me], d_ss, d_rs)
    for c in d_cp:
        c.start()
    send_pages(queue[ahead:])
    d_all[me] = d_send[me]

    @pl.loop(0, per_group)
    def _(r):
        for j in range(pages):
            rows[r, :, pl.ds(j * page, page), :] = pool[:, page_table[j, r]]

    fetch[7].wait()
    fetch[10].wait()
    entry_slot = [jnp.int32(r) for r in range(per_group)]
    entry_len = [cached_len[r] for r in range(per_group)]
    source = [jnp.int32(r) for r in range(per_group)]
    for d in range(1, groups):
        origin = lax.rem(me + groups - d, groups)
        count = jnp.int32(0)
        slots = [jnp.int32(0)] * move_cap
        for r in range(per_group):
            hit = meta_s[origin, 0, r] == me
            for k in range(move_cap):
                slots[k] = jnp.where(hit & (count == k), r, slots[k])
            source[r] = jnp.where(
                hit,
                per_group + (d - 1) * move_cap + jnp.minimum(count, move_cap - 1),
                source[r],
            )
            count = count + hit.astype(jnp.int32)
        for k in range(move_cap):
            entry_slot.append(slots[k])
            entry_len.append(meta_s[origin, 0, per_group + slots[k]])
    near = sorted(range(1, groups), key=lambda d: min(d, groups - d))
    late = [per_group + (d - 1) * move_cap + move_cap - 1 for d in near]
    told_row = lax.broadcasted_iota(jnp.int32, info.shape, 0)
    told_lane = lax.broadcasted_iota(jnp.int32, info.shape, 1)
    told = jnp.zeros(info.shape, jnp.int32)
    for r in range(per_group):
        told = jnp.where(told_row == r, source[r], told)
    for n, e in enumerate(late):
        counts = [(source[r] == e).astype(jnp.int32) for r in range(per_group)]
        real = functools.reduce(jnp.maximum, counts)
        told = jnp.where(
            told_row == per_group + n, jnp.where(told_lane == 1, real, entry_slot[e]), told
        )
    info[...] = told

    own_row = lax.broadcasted_iota(jnp.int32, (own_rows, sent_rows), 0)
    own_col = lax.broadcasted_iota(jnp.int32, (own_rows, sent_rows), 1)
    back = jnp.zeros((own_rows, sent_rows), jnp.int32)
    for r in range(per_group):
        back = jnp.where(own_row // steps == r, targets[r] + lax.rem(own_row, steps), back)
    back = (own_col == back).astype(f32).astype(bf16)
    ri = lax.broadcasted_iota(jnp.int32, (per_group * qr, per_kv * own_rows), 0)
    ci = lax.broadcasted_iota(jnp.int32, (per_group * qr, per_kv * own_rows), 1)
    place = (
        ci == (lax.rem(ri, qr) // steps) * own_rows + (ri // qr) * steps + lax.rem(ri, steps)
    )
    place = place.astype(f32).astype(bf16)
    base_rows = flat(frozen)

    for c in d_cp:
        c.wait_recv()
    d_in = d_all[...].astype(f32).reshape(sent_rows, width).astype(bf16)
    queries = base_rows + jnp.dot(back, d_in, preferred_element_type=f32)
    for h in range(kv_heads):
        stack = jnp.concatenate(
            [
                queries[:, (h * per_kv + i) * HEAD : (h * per_kv + i + 1) * HEAD]
                for i in range(per_kv)
            ],
            axis=0,
        ).astype(bf16)
        got = jnp.dot(place, stack, preferred_element_type=f32)
        q_rows[:, h] = got.reshape(per_group, qr, HEAD).astype(bf16)

    def cols(h):
        return slice(h * HEAD, (h + 1) * HEAD)

    def scored(items):
        work = []
        for entry, slot, length in items:
            new = [fresh[slot, t].astype(f32) for t in range(steps)]
            for h in range(kv_heads):
                pairs = [(n[0:1, cols(h)], n[1:2, cols(h)]) for n in new]
                work.append((q_rows[slot, h], rows[entry, 0, :, cols(h)], length, pairs))
        return probabilities(work, steps, qr)

    def arrived(slot, at, half):
        pltpu.make_async_remote_copy(
            src_ref=page_send.at[slot, at],
            dst_ref=rows.at[per_group + slot, at],
            send_sem=p_ss.at[slot, half],
            recv_sem=p_rs.at[slot, half],
            device_id=send_to(0),
            device_id_type=MESH,
        ).wait_recv()

    def attend(items):
        prob, added = scored(items)
        for n, (entry, h) in enumerate((i[0], h) for i in items for h in range(kv_heads)):
            part = prob[n * qr : (n + 1) * qr]
            o = jnp.dot(part, rows[entry, 1, :, cols(h)], preferred_element_type=f32)
            att[entry, h] = (o + added[n]).astype(bf16)

    for r in range(0, per_group, 4):
        attend([(e, e, entry_len[e]) for e in range(r, min(r + 4, per_group))])
    for k in range(move_cap - 1):
        for n in range(0, len(near), 3):
            items = []
            for d in near[n : n + 3]:
                slot = (d - 1) * move_cap + k
                arrived(slot, slice(None), 0)
                e = per_group + slot
                items.append((e, entry_slot[e], entry_len[e]))
            attend(items)
    for e in late:
        att[e] = jnp.zeros(att.shape[1:], bf16)
    pr = lax.broadcasted_iota(jnp.int32, (per_kv * own_rows, per_group * qr), 0)
    pc = lax.broadcasted_iota(jnp.int32, (per_kv * own_rows, per_group * qr), 1)
    in_row = lax.rem(pr, own_rows)
    spread = (
        pc == (in_row // steps) * qr + (pr // own_rows) * steps + lax.rem(in_row, steps)
    )
    spread = spread.astype(f32).astype(bf16)
    for h in range(kv_heads):
        stack = jnp.concatenate([att[source[r], h] for r in range(per_group)], axis=0)
        got = jnp.dot(spread, stack, preferred_element_type=f32)
        for i in range(per_kv):
            wide[:, (h * per_kv + i) * HEAD : (h * per_kv + i + 1) * HEAD] = got[
                i * own_rows : (i + 1) * own_rows
            ]
    for r in range(per_group):
        early[r] = wide[r * steps : (r + 1) * steps].astype(bf16)

    for n in range(0, len(near), 3):
        batch = late[n : n + 3]
        for e in batch:
            arrived(e - per_group, 0, 0)
        prob, added = scored([(e, entry_slot[e], entry_len[e]) for e in batch])
        for i, (j, h) in enumerate((j, h) for j in range(len(batch)) for h in range(kv_heads)):
            prob_last[n + j, h] = prob[i * qr : (i + 1) * qr]
            new_last[n + j, h] = added[i]

    for c in h_cp + m_cp + d_cp:
        c.wait_send()
    for d in range(1, mps):
        r_cp[d].wait_send()
    for p in p_cp.values():
        p.wait_send()
    for e in late:
        arrived(e - per_group, 1, 1)


def finish(cfg, rows, early, info, prob_last, new_last, att_out, cache_out, late, c_sem, e_sem):
    groups, mps, per_group, steps, block, store_count, rank, pages, page, move_cap = cfg
    f32, bf16 = jnp.float32, jnp.bfloat16
    last, kv_heads, qr, _ = new_last.shape
    per_kv = qr // steps
    told = info[...]
    source = [told[r, 0] for r in range(per_group)]
    out = [
        pltpu.make_async_copy(rows.at[source[r]], cache_out.at[:, r], c_sem.at[r])
        for r in range(per_group)
    ]
    for c in out:
        c.start()
    for r in range(per_group):
        from_last = (source[r] >= per_group) & (
            lax.rem(source[r] - per_group, move_cap) == move_cap - 1
        )

        @pl.when(jnp.logical_not(from_last))
        def _():
            pltpu.make_async_copy(early.at[r], att_out.at[r], e_sem.at[r]).start()

    near = sorted(range(1, groups), key=lambda d: min(d, groups - d))
    entry = [per_group + (d - 1) * move_cap + move_cap - 1 for d in near]
    for n in range(last):
        for h in range(kv_heads):
            values = rows[entry[n], 1, :, h * HEAD : (h + 1) * HEAD]
            o = new_last[n, h] + jnp.dot(prob_last[n, h], values, preferred_element_type=f32)
            for i in range(per_kv):
                late[n, :, (h * per_kv + i) * HEAD : (h * per_kv + i + 1) * HEAD] = o[
                    i * steps : (i + 1) * steps
                ].astype(bf16)
    for n in range(last):
        slot = told[per_group + n, 0]

        @pl.when(told[per_group + n, 1] == 1)
        def _():
            pltpu.make_async_copy(late.at[n], att_out.at[slot], e_sem.at[slot]).start()

    for r in range(per_group):
        out.append(pltpu.make_async_copy(early.at[r], att_out.at[r], e_sem.at[r]))
    for c in out:
        c.wait()


def per_device(
    hidden_in,
    frozen_query_rows,
    new_kv,
    adapter_of,
    adapter_home,
    a_store,
    b_store,
    kv_pool,
    page_table,
    cached_len,
    new_group,
):
    groups = lax.axis_size("req")
    mps = lax.axis_size("mp")
    per_group, steps, width = hidden_in.shape
    store_count, rank, _ = a_store.shape
    pages, page = page_table.shape[1], kv_pool.shape[2]
    kv_width = kv_pool.shape[3]
    context = pages * page
    move_cap = -(-(per_group - per_group // 4) // groups)
    cap = -(-per_group // min(16, groups))
    block = -(-cap * steps // 8) * 8
    lanes = store_count * rank
    qr = width // kv_width * steps
    kv_heads = kv_width // HEAD
    moved = (groups - 1) * move_cap
    last = groups - 1
    entries = per_group + moved
    bf16, f32, i32 = jnp.bfloat16, jnp.float32, jnp.int32
    cfg = (groups, mps, per_group, steps, block, store_count, rank, pages, page, move_cap)
    dma = pltpu.SemaphoreType.DMA
    given = (
        adapter_of,
        adapter_home,
        page_table.T,
        cached_len,
        new_group,
        hidden_in,
        kv_pool,
        frozen_query_rows,
        a_store.reshape(lanes, width),
        b_store.reshape(lanes, width),
        new_kv,
    )
    passed = (
        jax.ShapeDtypeStruct((entries, 2, context, kv_width), bf16),
        jax.ShapeDtypeStruct((per_group, steps, width), bf16),
        jax.ShapeDtypeStruct((-(-(per_group + last) // 8) * 8, 128), i32),
        jax.ShapeDtypeStruct((last, kv_heads, qr, context), bf16),
        jax.ShapeDtypeStruct((last, kv_heads, qr, HEAD), f32),
    )
    scratch = [
        VMEM((groups, block, width), bf16),
        VMEM((groups, block, width), bf16),
        VMEM((groups * block, lanes), f32),
        VMEM((mps, groups * block, lanes), f32),
        VMEM((groups, block, width), bf16),
        VMEM((groups, block, width), bf16),
        VMEM((per_group, kv_heads, qr, HEAD), bf16),
        VMEM((per_group * steps, width), f32),
        VMEM((1, 128), i32),
        VMEM((groups, 1, 128), i32),
        SMEM((groups, 1, 128), i32),
        VMEM((moved, 2, context, kv_width), bf16),
        VMEM((entries, kv_heads, qr, HEAD), bf16),
        dma((groups - 1,)),
        dma((groups - 1,)),
        dma((mps - 1,)),
        dma((mps - 1,)),
        dma((groups - 1,)),
        dma((groups - 1,)),
        dma((groups - 1,)),
        dma((groups - 1,)),
        dma((moved, 2)),
        dma((moved, 2)),
        dma,
        pltpu.SemaphoreType.REGULAR((groups,)),
        pltpu.SemaphoreType.REGULAR,
        pltpu.SemaphoreType.REGULAR,
    ]

    def first(*refs):
        n = len(given)
        held = n + len(passed)
        exchange(
            cfg, refs[:n], refs[n:held], refs[held : held + n], refs[held + n], *refs[held + n + 1 :]
        )

    between = pl.pallas_call(
        first,
        out_shape=passed,
        in_specs=[pl.BlockSpec(memory_space=HBM)] * len(given),
        out_specs=[pl.BlockSpec(memory_space=VMEM)] * len(passed),
        scratch_shapes=[SMEM(g.shape, g.dtype) for g in given[:5]]
        + [VMEM(g.shape, g.dtype) for g in given[5:]]
        + [dma((len(given),))]
        + scratch,
        compiler_params=pltpu.CompilerParams(
            collective_id=0, has_side_effects=True, vmem_limit_bytes=32 * 2**20
        ),
        name="exchange",
    )(*[pltpu.with_memory_space_constraint(g, HBM) for g in given])
    return pl.pallas_call(
        functools.partial(finish, cfg),
        out_shape=(
            jax.ShapeDtypeStruct((per_group, steps, width), bf16),
            jax.ShapeDtypeStruct((2, per_group, context, kv_width), bf16),
        ),
        in_specs=[
            pl.BlockSpec(memory_space=m) for m in (VMEM, VMEM, VMEM, VMEM, VMEM)
        ],
        out_specs=[pl.BlockSpec(memory_space=HBM)] * 2,
        scratch_shapes=[
            VMEM((last, steps, width), bf16),
            dma((per_group,)),
            dma((per_group,)),
        ],
        compiler_params=pltpu.CompilerParams(vmem_limit_bytes=16 * 2**20),
        name="finish",
    )(*between)


def solution(mesh):
    placed = (
        P(("rep", "req"), None, "mp"),
        P(("rep", "req"), None, "mp"),
        P(("rep", "req"), None, None, "mp"),
        P(("rep", "req")),
        P("rep"),
        P(("rep", "req"), None, "mp"),
        P(("rep", "req"), None, "mp"),
        P(None, ("rep", "req"), None, "mp"),
        P(("rep", "req"), None),
        P(("rep", "req")),
        P(("rep", "req")),
    )
    return jax.shard_map(
        per_device,
        mesh=mesh,
        in_specs=placed,
        out_specs=(P(("rep", "req"), None, "mp"), P(None, ("rep", "req"), None, "mp")),
        check_vma=False,
    )
```

```python
import functools

import jax
import jax.numpy as jnp
from jax import lax
from jax.experimental import pallas as pl
from jax.experimental.pallas import tpu as pltpu
from jax.sharding import PartitionSpec as P

HEAD = 128
NEG_FILL = -1e30
MESH = pl.DeviceIdType.MESH
VMEM = pltpu.VMEM
SMEM = pltpu.SMEM
HBM = pltpu.HBM


def probabilities(work, steps, qr):
    f32, bf16 = jnp.float32, jnp.bfloat16
    scale = HEAD ** (-0.5)
    context = work[0][1].shape[0]
    position = lax.broadcasted_iota(jnp.int32, (qr, context), 1)
    scores, extra = [], []
    for q, keys, length, fresh in work:
        s = lax.dot_general(q, keys, (((1,), (1,)), ((), ())), preferred_element_type=f32)
        scores.append(jnp.where(position < length, s * scale, NEG_FILL))
        qf = q.astype(f32)
        extra.append([jnp.sum(qf * fresh[t][0], axis=1, keepdims=True) for t in range(steps)])
    scores = jnp.concatenate(scores, axis=0)
    step_of = lax.rem(lax.broadcasted_iota(jnp.int32, (len(work) * qr, 1), 0), steps)
    extra = [
        jnp.where(
            step_of >= t, jnp.concatenate([e[t] for e in extra], axis=0) * scale, NEG_FILL
        )
        for t in range(steps)
    ]
    top = jnp.max(scores, axis=1, keepdims=True)
    for e in extra:
        top = jnp.maximum(top, e)
    weights = jnp.exp(scores - top)
    extra = [jnp.exp(e - top) for e in extra]
    norm = jnp.sum(weights, axis=1, keepdims=True)
    for e in extra:
        norm = norm + e
    prob = (weights / norm).astype(bf16)
    extra = [(e / norm).astype(bf16).astype(f32) for e in extra]
    added = []
    for n, (_, _, _, fresh) in enumerate(work):
        part = slice(n * qr, (n + 1) * qr)
        o = extra[0][part] * fresh[0][1]
        for t in range(1, steps):
            o = o + extra[t][part] * fresh[t][1]
        added.append(o)
    return prob, added


def exchange(
    cfg,
    given,
    outs,
    held,
    in_sem,
    h_send,
    h_all,
    r_part,
    r_all,
    d_send,
    d_all,
    q_rows,
    wide,
    meta_send,
    meta_all,
    meta_s,
    page_send,
    att,
    h_ss,
    h_rs,
    r_ss,
    r_rs,
    d_ss,
    d_rs,
    m_ss,
    m_rs,
    p_ss,
    p_rs,
    l_sem,
    here,
    columns,
    everyone,
):
    groups, mps, per_group, steps, block, store_count, rank, pages, page, move_cap = cfg
    rows, early, info, prob_last, new_last = outs
    f32, bf16 = jnp.float32, jnp.bfloat16
    rep = lax.axis_index("rep")
    me = lax.axis_index("req")
    mp = lax.axis_index("mp")
    fetch = [
        pltpu.make_async_copy(src, dst, in_sem.at[i])
        for i, (src, dst) in enumerate(zip(given, held))
    ]
    for f in fetch:
        f.start()
    (
        adapter_of,
        adapter_home,
        page_table,
        cached_len,
        new_group,
        hidden,
        pool,
        frozen,
        a_panels,
        b_panels,
        fresh,
    ) = held
    width = hidden.shape[2]
    lanes = store_count * rank
    kv_width = pool.shape[3]
    kv_heads = kv_width // HEAD
    per_kv = width // kv_width
    sent_rows = groups * block
    own_rows = per_group * steps
    qr = per_kv * steps

    upper = me // (groups // 2)

    def target(j):
        down = groups - 1 - j
        down = down - jnp.clip(me - down + 1, 0, 1)
        up = j + jnp.clip(j - me + 1, 0, 1)
        return down + upper * (up - down)

    def step_to(j):
        return lax.rem(target(j) - me + groups, groups)

    def send_to(j):
        return (rep, target(j), mp)

    barrier = pltpu.get_barrier_semaphore()
    beside = [(rep, me, lax.rem(mp + d, mps)) for d in range(1, mps)]
    for t in range(1, groups):

        @pl.when(me < t)
        def _():
            pl.semaphore_signal(barrier, inc=1, device_id=(rep, t, mp), device_id_type=MESH)

    @pl.when(me == 0)
    def _():
        for device in beside:
            pl.semaphore_signal(barrier, inc=1, device_id=device, device_id_type=MESH)

    @pl.when(me > 0)
    def _():
        pl.semaphore_wait(barrier, me)

    for t in range(groups - 1):

        @pl.when(me > t)
        def _():
            pl.semaphore_signal(
                here.at[me], inc=1, device_id=(rep, t, mp), device_id_type=MESH
            )

    def flat(ref):
        for r in range(per_group):
            wide[r * steps : (r + 1) * steps] = ref[r].astype(f32)
        return wide[...]

    fetch[5].wait()
    hidden_rows = flat(hidden).astype(bf16)
    for f in fetch[:5]:
        f.wait()

    homes = [adapter_home[adapter_of[r]] for r in range(per_group)]
    square = (own_rows, own_rows)
    of_row = lax.broadcasted_iota(jnp.int32, square, 0)
    of_col = lax.broadcasted_iota(jnp.int32, square, 1)
    owner_row = jnp.zeros(square, jnp.int32)
    owner_col = jnp.zeros((1, own_rows), jnp.int32)
    one_row = lax.broadcasted_iota(jnp.int32, (1, own_rows), 1)
    for r in range(per_group):
        owner_row = jnp.where(of_row // steps == r, homes[r], owner_row)
        owner_col = jnp.where(one_row // steps == r, homes[r], owner_col)
    owner_row, owner_col = owner_row // store_count, owner_col // store_count
    before = (owner_row == owner_col) & (of_row // steps < of_col // steps)
    placed = jnp.sum(before.astype(f32), axis=0, keepdims=True).astype(jnp.int32)
    want = owner_col * block + placed + lax.rem(one_row, steps)
    sent_row = lax.broadcasted_iota(jnp.int32, (sent_rows, own_rows), 0)
    pick_by_owner = (sent_row == want).astype(f32).astype(bf16)
    h_out = jnp.dot(pick_by_owner, hidden_rows, preferred_element_type=f32)
    h_send[...] = h_out.reshape(groups, block, width).astype(bf16)

    def copies(src, dst, ss, rs):
        out = []
        for j in range(groups - 1):
            d = step_to(j)
            out.append(
                pltpu.make_async_remote_copy(
                    src_ref=src(target(j)),
                    dst_ref=dst,
                    send_sem=ss.at[d - 1],
                    recv_sem=rs.at[d - 1],
                    device_id=send_to(j),
                    device_id_type=MESH,
                )
            )
        return out

    h_cp = copies(lambda t: h_send.at[t], h_all.at[me], h_ss, h_rs)

    for t in range(1, groups - 1):

        @pl.when(me < t)
        def _():
            pl.semaphore_wait(here.at[t], 1)

    @pl.when(upper == 0)
    def _():
        for c in h_cp[1:]:
            c.start()

    @pl.when(upper == 1)
    def _():
        for c in h_cp[:-1]:
            c.start()

    h_all[me] = h_send[me]

    lane = lax.broadcasted_iota(jnp.int32, (1, 128), 1)
    meta = jnp.zeros((1, 128), jnp.int32)
    for r in range(per_group):
        meta = jnp.where(lane == r, new_group[r], meta)
        meta = jnp.where(lane == per_group + r, cached_len[r], meta)
        owner = homes[r] // store_count
        pick = homes[r] - owner * store_count
        meta = jnp.where(lane == 2 * per_group + owner, pick, meta)
    meta_send[...] = meta
    m_cp = copies(lambda t: meta_send, meta_all.at[me], m_ss, m_rs)
    meta_all[me] = meta

    fetch[6].wait()
    sources = []
    for j in range(groups - 1):
        dest = target(j)
        count = jnp.int32(0)
        picked = [jnp.int32(0)] * move_cap
        for r in range(per_group):
            hit = new_group[r] == dest
            for k in range(move_cap):
                picked[k] = jnp.where(hit & (count == k), r, picked[k])
            count = count + hit.astype(jnp.int32)
        sources.append(picked)

    p_cp = {}

    def pack_pages(k, peers):
        for j in peers:
            slot = (step_to(j) - 1) * move_cap + k
            for i in range(pages):
                page_id = page_table[i, sources[j][k]]
                page_send[slot, :, pl.ds(i * page, page), :] = pool[:, page_id]
            for half in range(2):
                at = slice(None) if k < move_cap - 1 else half
                p_cp[j, k, half] = pltpu.make_async_remote_copy(
                    src_ref=page_send.at[slot, at],
                    dst_ref=rows.at[per_group + slot, at],
                    send_sem=p_ss.at[slot, half],
                    recv_sem=p_rs.at[slot, half],
                    device_id=send_to(j),
                    device_id_type=MESH,
                )
                if k < move_cap - 1:
                    break

    others = range(groups - 1)
    queue = [(j, 0) for j in others] + [(0, k) for k in range(1, move_cap)]
    queue += [(j, k) for k in range(1, move_cap) for j in others[:0:-1]]
    ahead = groups if move_cap > 1 else groups // 2

    def send_pages(some):
        for j, k in some:
            for half in range(1 if k < move_cap - 1 else 2):
                p_cp[j, k, half].start()

    first = [s for s in queue[:ahead] if s[1] == 0]
    straight = groups // 2 - 1
    pack_pages(0, [straight])
    send_pages([s for s in first if s[0] == straight])

    @pl.when(me < groups - 1)
    def _():
        pl.semaphore_wait(here.at[groups - 1], 1)

    @pl.when(upper == 0)
    def _():
        h_cp[0].start()

    @pl.when(upper == 1)
    def _():
        h_cp[-1].start()

    for c in m_cp:
        c.start()
    pack_pages(0, [j for j in others if j != straight])
    send_pages([s for s in first if s[0] != straight])

    @pl.when(me == 0)
    def _():
        pl.semaphore_wait(barrier, mps - 1)
        for device in beside:
            pl.semaphore_signal(columns, inc=1, device_id=device, device_id_type=MESH)
        pl.semaphore_wait(columns, mps - 1)
        for t in range(1, groups):
            pl.semaphore_signal(everyone, inc=1, device_id=(rep, t, mp), device_id_type=MESH)

    @pl.when(me > 0)
    def _():
        pl.semaphore_wait(everyone, 1)

    fetch[8].wait()
    for c in h_cp:
        c.wait_recv()
    h_in = h_all[...].astype(f32).reshape(sent_rows, width).astype(bf16)
    r_part[...] = lax.dot_general(
        h_in, a_panels[...], (((1,), (1,)), ((), ())), preferred_element_type=f32
    )
    r_cp = {}
    for d in range(1, mps):
        r_cp[d] = pltpu.make_async_remote_copy(
            src_ref=r_part,
            dst_ref=r_all.at[mp],
            send_sem=r_ss.at[d - 1],
            recv_sem=r_rs.at[d - 1],
            device_id=(rep, me, lax.rem(mp + d, mps)),
            device_id_type=MESH,
        )
        r_cp[d].start()
    r_all[mp] = r_part[...]

    for c in m_cp:
        c.wait_recv()
    local = pltpu.make_async_copy(meta_all, meta_s, l_sem)
    local.start()

    for k in range(1, move_cap):
        pack_pages(k, others)
    send_pages([s for s in queue[:ahead] if s[1] > 0])

    local.wait()
    mrow = lax.broadcasted_iota(jnp.int32, (sent_rows, lanes), 0) // block
    mlane = lax.broadcasted_iota(jnp.int32, (sent_rows, lanes), 1) // rank
    wanted = jnp.zeros((sent_rows, lanes), jnp.int32)
    for g in range(groups):
        wanted = jnp.where(mrow == g, meta_s[g, 0, 2 * per_group + me], wanted)

    fetch[9].wait()
    for d in range(1, mps):
        r_cp[d].wait_recv()
    total = r_all[0]
    for j in range(1, mps):
        total = total + r_all[j]
    total = jnp.where(mlane == wanted, total, 0.0).astype(bf16)
    delta = jnp.dot(total, b_panels[...], preferred_element_type=f32)
    d_send[...] = delta.reshape(groups, block, width).astype(bf16)
    d_cp = copies(lambda t: d_send.at[t], d_all.at[me], d_ss, d_rs)
    for c in d_cp:
        c.start()
    send_pages(queue[ahead:])
    d_all[me] = d_send[me]

    @pl.loop(0, per_group)
    def _(r):
        for j in range(pages):
            rows[r, :, pl.ds(j * page, page), :] = pool[:, page_table[j, r]]

    fetch[7].wait()
    fetch[10].wait()
    entry_slot = [jnp.int32(r) for r in range(per_group)]
    entry_len = [cached_len[r] for r in range(per_group)]
    source = [jnp.int32(r) for r in range(per_group)]
    for d in range(1, groups):
        origin = lax.rem(me + groups - d, groups)
        count = jnp.int32(0)
        slots = [jnp.int32(0)] * move_cap
        for r in range(per_group):
            hit = meta_s[origin, 0, r] == me
            for k in range(move_cap):
                slots[k] = jnp.where(hit & (count == k), r, slots[k])
            source[r] = jnp.where(
                hit,
                per_group + (d - 1) * move_cap + jnp.minimum(count, move_cap - 1),
                source[r],
            )
            count = count + hit.astype(jnp.int32)
        for k in range(move_cap):
            entry_slot.append(slots[k])
            entry_len.append(meta_s[origin, 0, per_group + slots[k]])
    near = sorted(range(1, groups), key=lambda d: min(d, groups - d))
    late = [per_group + (d - 1) * move_cap + move_cap - 1 for d in near]
    words = []
    for r in range(0, per_group, 4):
        words.append(sum(s << (8 * i) for i, s in enumerate(source[r : r + 4])))
    for e in late:
        real = functools.reduce(jnp.maximum, [(s == e).astype(jnp.int32) for s in source])
        words.append(entry_slot[e] * 2 + real)
    told_row = lax.broadcasted_iota(jnp.int32, info.shape, 0)
    told = jnp.zeros(info.shape, jnp.int32)
    for i, word in enumerate(words):
        told = jnp.where(told_row == i, word, told)
    info[...] = told

    ri = lax.broadcasted_iota(jnp.int32, (per_group * qr, per_kv * own_rows), 0)
    ci = lax.broadcasted_iota(jnp.int32, (per_group * qr, per_kv * own_rows), 1)
    place = (
        ci == (lax.rem(ri, qr) // steps) * own_rows + (ri // qr) * steps + lax.rem(ri, steps)
    )
    place = place.astype(f32).astype(bf16)
    base_rows = flat(frozen)

    for c in d_cp:
        c.wait_recv()
    d_in = d_all[...].astype(f32).reshape(sent_rows, width).astype(bf16)
    queries = base_rows + lax.dot_general(
        pick_by_owner, d_in, (((0,), (0,)), ((), ())), preferred_element_type=f32
    )
    for h in range(kv_heads):
        stack = jnp.concatenate(
            [
                queries[:, (h * per_kv + i) * HEAD : (h * per_kv + i + 1) * HEAD]
                for i in range(per_kv)
            ],
            axis=0,
        ).astype(bf16)
        got = jnp.dot(place, stack, preferred_element_type=f32)
        q_rows[:, h] = got.reshape(per_group, qr, HEAD).astype(bf16)

    def cols(h):
        return slice(h * HEAD, (h + 1) * HEAD)

    def scored(items):
        work = []
        for entry, slot, length in items:
            new = [fresh[slot, t].astype(f32) for t in range(steps)]
            for h in range(kv_heads):
                pairs = [(n[0:1, cols(h)], n[1:2, cols(h)]) for n in new]
                work.append((q_rows[slot, h], rows[entry, 0, :, cols(h)], length, pairs))
        return probabilities(work, steps, qr)

    def arrived(slot, at, half):
        pltpu.make_async_remote_copy(
            src_ref=page_send.at[slot, at],
            dst_ref=rows.at[per_group + slot, at],
            send_sem=p_ss.at[slot, half],
            recv_sem=p_rs.at[slot, half],
            device_id=send_to(0),
            device_id_type=MESH,
        ).wait_recv()

    def attend(items):
        prob, added = scored(items)
        for n, (entry, h) in enumerate((i[0], h) for i in items for h in range(kv_heads)):
            part = prob[n * qr : (n + 1) * qr]
            o = jnp.dot(part, rows[entry, 1, :, cols(h)], preferred_element_type=f32)
            att[entry, h] = (o + added[n]).astype(bf16)

    for r in range(0, per_group, 4):
        attend([(e, e, entry_len[e]) for e in range(r, min(r + 4, per_group))])
    for k in range(move_cap - 1):
        for n in range(0, len(near), 3):
            items = []
            for d in near[n : n + 3]:
                slot = (d - 1) * move_cap + k
                arrived(slot, slice(None), 0)
                e = per_group + slot
                items.append((e, entry_slot[e], entry_len[e]))
            attend(items)
    for e in late:
        att[e] = jnp.zeros(att.shape[1:], bf16)
    pr = lax.broadcasted_iota(jnp.int32, (per_kv * own_rows, per_group * qr), 0)
    pc = lax.broadcasted_iota(jnp.int32, (per_kv * own_rows, per_group * qr), 1)
    in_row = lax.rem(pr, own_rows)
    spread = (
        pc == (in_row // steps) * qr + (pr // own_rows) * steps + lax.rem(in_row, steps)
    )
    spread = spread.astype(f32).astype(bf16)
    for h in range(kv_heads):
        stack = jnp.concatenate([att[source[r], h] for r in range(per_group)], axis=0)
        got = jnp.dot(spread, stack, preferred_element_type=f32)
        for i in range(per_kv):
            wide[:, (h * per_kv + i) * HEAD : (h * per_kv + i + 1) * HEAD] = got[
                i * own_rows : (i + 1) * own_rows
            ]
    for r in range(per_group):
        early[r] = wide[r * steps : (r + 1) * steps].astype(bf16)

    for n in range(0, len(near), 3):
        batch = late[n : n + 3]
        for e in batch:
            arrived(e - per_group, 0, 0)
        prob, added = scored([(e, entry_slot[e], entry_len[e]) for e in batch])
        for i, (j, h) in enumerate((j, h) for j in range(len(batch)) for h in range(kv_heads)):
            prob_last[n + j, h] = prob[i * qr : (i + 1) * qr]
            new_last[n + j, h] = added[i]

    for c in h_cp + m_cp + d_cp:
        c.wait_send()
    for d in range(1, mps):
        r_cp[d].wait_send()
    for p in p_cp.values():
        p.wait_send()
    for e in late:
        arrived(e - per_group, 1, 1)


def finish(cfg, rows, early, info, prob_last, new_last, att_out, cache_out, late, c_sem, e_sem):
    groups, mps, per_group, steps, block, store_count, rank, pages, page, move_cap = cfg
    f32, bf16 = jnp.float32, jnp.bfloat16
    last, kv_heads, qr, _ = new_last.shape
    per_kv = qr // steps
    told = info[...]
    words = -(-per_group // 4)
    source = [(told[r // 4, 0] >> (8 * (r % 4))) & 255 for r in range(per_group)]
    out = [
        pltpu.make_async_copy(rows.at[source[r]], cache_out.at[:, r], c_sem.at[r])
        for r in range(per_group)
    ]
    for c in out:
        c.start()
    for r in range(per_group):
        from_last = (source[r] >= per_group) & (
            lax.rem(source[r] - per_group, move_cap) == move_cap - 1
        )

        @pl.when(jnp.logical_not(from_last))
        def _():
            pltpu.make_async_copy(early.at[r], att_out.at[r], e_sem.at[r]).start()

    near = sorted(range(1, groups), key=lambda d: min(d, groups - d))
    entry = [per_group + (d - 1) * move_cap + move_cap - 1 for d in near]
    for n in range(last):
        for h in range(kv_heads):
            values = rows[entry[n], 1, :, h * HEAD : (h + 1) * HEAD]
            o = new_last[n, h] + jnp.dot(prob_last[n, h], values, preferred_element_type=f32)
            for i in range(per_kv):
                late[n, :, (h * per_kv + i) * HEAD : (h * per_kv + i + 1) * HEAD] = o[
                    i * steps : (i + 1) * steps
                ].astype(bf16)
    for n in range(last):
        word = told[words + n, 0]
        slot = word // 2

        @pl.when(lax.rem(word, 2) == 1)
        def _():
            pltpu.make_async_copy(late.at[n], att_out.at[slot], e_sem.at[slot]).start()

    for r in range(per_group):
        out.append(pltpu.make_async_copy(early.at[r], att_out.at[r], e_sem.at[r]))
    for c in out:
        c.wait()


def per_device(
    hidden_in,
    frozen_query_rows,
    new_kv,
    adapter_of,
    adapter_home,
    a_store,
    b_store,
    kv_pool,
    page_table,
    cached_len,
    new_group,
):
    groups = lax.axis_size("req")
    mps = lax.axis_size("mp")
    per_group, steps, width = hidden_in.shape
    store_count, rank, _ = a_store.shape
    pages, page = page_table.shape[1], kv_pool.shape[2]
    kv_width = kv_pool.shape[3]
    context = pages * page
    move_cap = -(-(per_group - per_group // 4) // groups)
    cap = -(-per_group // min(16, groups))
    block = -(-cap * steps // 8) * 8
    lanes = store_count * rank
    qr = width // kv_width * steps
    kv_heads = kv_width // HEAD
    moved = (groups - 1) * move_cap
    last = groups - 1
    entries = per_group + moved
    bf16, f32, i32 = jnp.bfloat16, jnp.float32, jnp.int32
    cfg = (groups, mps, per_group, steps, block, store_count, rank, pages, page, move_cap)
    dma = pltpu.SemaphoreType.DMA
    given = (
        adapter_of,
        adapter_home,
        page_table.T,
        cached_len,
        new_group,
        hidden_in,
        kv_pool,
        frozen_query_rows,
        a_store.reshape(lanes, width),
        b_store.reshape(lanes, width),
        new_kv,
    )
    passed = (
        jax.ShapeDtypeStruct((entries, 2, context, kv_width), bf16),
        jax.ShapeDtypeStruct((per_group, steps, width), bf16),
        jax.ShapeDtypeStruct((-(-(-(-per_group // 4) + last) // 8) * 8, 128), i32),
        jax.ShapeDtypeStruct((last, kv_heads, qr, context), bf16),
        jax.ShapeDtypeStruct((last, kv_heads, qr, HEAD), f32),
    )
    scratch = [
        VMEM((groups, block, width), bf16),
        VMEM((groups, block, width), bf16),
        VMEM((groups * block, lanes), f32),
        VMEM((mps, groups * block, lanes), f32),
        VMEM((groups, block, width), bf16),
        VMEM((groups, block, width), bf16),
        VMEM((per_group, kv_heads, qr, HEAD), bf16),
        VMEM((per_group * steps, width), f32),
        VMEM((1, 128), i32),
        VMEM((groups, 1, 128), i32),
        SMEM((groups, 1, 128), i32),
        VMEM((moved, 2, context, kv_width), bf16),
        VMEM((entries, kv_heads, qr, HEAD), bf16),
        dma((groups - 1,)),
        dma((groups - 1,)),
        dma((mps - 1,)),
        dma((mps - 1,)),
        dma((groups - 1,)),
        dma((groups - 1,)),
        dma((groups - 1,)),
        dma((groups - 1,)),
        dma((moved, 2)),
        dma((moved, 2)),
        dma,
        pltpu.SemaphoreType.REGULAR((groups,)),
        pltpu.SemaphoreType.REGULAR,
        pltpu.SemaphoreType.REGULAR,
    ]

    def first(*refs):
        n = len(given)
        held = n + len(passed)
        exchange(
            cfg, refs[:n], refs[n:held], refs[held : held + n], refs[held + n], *refs[held + n + 1 :]
        )

    between = pl.pallas_call(
        first,
        out_shape=passed,
        in_specs=[pl.BlockSpec(memory_space=HBM)] * len(given),
        out_specs=[pl.BlockSpec(memory_space=VMEM)] * len(passed),
        scratch_shapes=[SMEM(g.shape, g.dtype) for g in given[:5]]
        + [VMEM(g.shape, g.dtype) for g in given[5:]]
        + [dma((len(given),))]
        + scratch,
        compiler_params=pltpu.CompilerParams(
            collective_id=0, has_side_effects=True, vmem_limit_bytes=32 * 2**20
        ),
        name="exchange",
    )(*[pltpu.with_memory_space_constraint(g, HBM) for g in given])
    return pl.pallas_call(
        functools.partial(finish, cfg),
        out_shape=(
            jax.ShapeDtypeStruct((per_group, steps, width), bf16),
            jax.ShapeDtypeStruct((2, per_group, context, kv_width), bf16),
        ),
        in_specs=[
            pl.BlockSpec(memory_space=m) for m in (VMEM, VMEM, VMEM, VMEM, VMEM)
        ],
        out_specs=[pl.BlockSpec(memory_space=HBM)] * 2,
        scratch_shapes=[
            VMEM((last, steps, width), bf16),
            dma((per_group,)),
            dma((per_group,)),
        ],
        compiler_params=pltpu.CompilerParams(vmem_limit_bytes=16 * 2**20),
        name="finish",
    )(*between)


def solution(mesh):
    placed = (
        P(("rep", "req"), None, "mp"),
        P(("rep", "req"), None, "mp"),
        P(("rep", "req"), None, None, "mp"),
        P(("rep", "req")),
        P("rep"),
        P(("rep", "req"), None, "mp"),
        P(("rep", "req"), None, "mp"),
        P(None, ("rep", "req"), None, "mp"),
        P(("rep", "req"), None),
        P(("rep", "req")),
        P(("rep", "req")),
    )
    return jax.shard_map(
        per_device,
        mesh=mesh,
        in_specs=placed,
        out_specs=(P(("rep", "req"), None, "mp"), P(None, ("rep", "req"), None, "mp")),
        check_vma=False,
    )
```

```python
import functools

import jax
import jax.numpy as jnp
from jax import lax
from jax.experimental import pallas as pl
from jax.experimental.pallas import tpu as pltpu
from jax.sharding import PartitionSpec as P

HEAD = 128
NEG_FILL = -1e30
MESH = pl.DeviceIdType.MESH
VMEM = pltpu.VMEM
SMEM = pltpu.SMEM
HBM = pltpu.HBM


def probabilities(work, steps, qr):
    f32, bf16 = jnp.float32, jnp.bfloat16
    scale = HEAD ** (-0.5)
    context = work[0][1].shape[0]
    position = lax.broadcasted_iota(jnp.int32, (qr, context), 1)
    scores, extra = [], []
    for q, keys, length, fresh in work:
        s = lax.dot_general(q, keys, (((1,), (1,)), ((), ())), preferred_element_type=f32)
        scores.append(jnp.where(position < length, s * scale, NEG_FILL))
        qf = q.astype(f32)
        extra.append([jnp.sum(qf * fresh[t][0], axis=1, keepdims=True) for t in range(steps)])
    scores = jnp.concatenate(scores, axis=0)
    step_of = lax.rem(lax.broadcasted_iota(jnp.int32, (len(work) * qr, 1), 0), steps)
    extra = [
        jnp.where(
            step_of >= t, jnp.concatenate([e[t] for e in extra], axis=0) * scale, NEG_FILL
        )
        for t in range(steps)
    ]
    top = jnp.max(scores, axis=1, keepdims=True)
    for e in extra:
        top = jnp.maximum(top, e)
    weights = jnp.exp(scores - top)
    extra = [jnp.exp(e - top) for e in extra]
    norm = jnp.sum(weights, axis=1, keepdims=True)
    for e in extra:
        norm = norm + e
    prob = (weights / norm).astype(bf16)
    extra = [(e / norm).astype(bf16).astype(f32) for e in extra]
    added = []
    for n, (_, _, _, fresh) in enumerate(work):
        part = slice(n * qr, (n + 1) * qr)
        o = extra[0][part] * fresh[0][1]
        for t in range(1, steps):
            o = o + extra[t][part] * fresh[t][1]
        added.append(o)
    return prob, added


def exchange(
    cfg,
    given,
    outs,
    held,
    in_sem,
    h_send,
    h_all,
    r_part,
    r_all,
    d_send,
    d_all,
    q_rows,
    wide,
    meta_send,
    meta_all,
    meta_s,
    page_send,
    att,
    h_ss,
    h_rs,
    r_ss,
    r_rs,
    d_ss,
    d_rs,
    m_ss,
    m_rs,
    p_ss,
    p_rs,
    l_sem,
    here,
    columns,
    everyone,
):
    groups, mps, per_group, steps, block, store_count, rank, pages, page, move_cap = cfg
    rows, early, info, prob_last, new_last = outs
    f32, bf16 = jnp.float32, jnp.bfloat16
    rep = lax.axis_index("rep")
    me = lax.axis_index("req")
    mp = lax.axis_index("mp")
    fetch = [
        pltpu.make_async_copy(src, dst, in_sem.at[i])
        for i, (src, dst) in enumerate(zip(given, held))
    ]
    for f in fetch[:6]:
        f.start()
    (
        adapter_of,
        adapter_home,
        page_table,
        cached_len,
        new_group,
        hidden,
        pool,
        frozen,
        a_panels,
        b_panels,
        fresh,
    ) = held
    width = hidden.shape[2]
    lanes = store_count * rank
    kv_width = pool.shape[3]
    kv_heads = kv_width // HEAD
    per_kv = width // kv_width
    sent_rows = groups * block
    own_rows = per_group * steps
    qr = per_kv * steps

    upper = me // (groups // 2)

    def target(j):
        down = groups - 1 - j
        down = down - jnp.clip(me - down + 1, 0, 1)
        up = j + jnp.clip(j - me + 1, 0, 1)
        return down + upper * (up - down)

    def step_to(j):
        return lax.rem(target(j) - me + groups, groups)

    def send_to(j):
        return (rep, target(j), mp)

    barrier = pltpu.get_barrier_semaphore()
    beside = [(rep, me, lax.rem(mp + d, mps)) for d in range(1, mps)]
    for t in range(1, groups):

        @pl.when(me < t)
        def _():
            pl.semaphore_signal(barrier, inc=1, device_id=(rep, t, mp), device_id_type=MESH)

    @pl.when(me == 0)
    def _():
        for device in beside:
            pl.semaphore_signal(barrier, inc=1, device_id=device, device_id_type=MESH)

    @pl.when(me > 0)
    def _():
        pl.semaphore_wait(barrier, me)

    for t in range(groups - 1):

        @pl.when(me > t)
        def _():
            pl.semaphore_signal(
                here.at[me], inc=1, device_id=(rep, t, mp), device_id_type=MESH
            )

    for f in fetch[6:]:
        f.start()

    def flat(ref):
        for r in range(per_group):
            wide[r * steps : (r + 1) * steps] = ref[r].astype(f32)
        return wide[...]

    fetch[5].wait()
    hidden_rows = flat(hidden).astype(bf16)
    for f in fetch[:5]:
        f.wait()

    homes = [adapter_home[adapter_of[r]] for r in range(per_group)]
    square = (own_rows, own_rows)
    of_row = lax.broadcasted_iota(jnp.int32, square, 0)
    of_col = lax.broadcasted_iota(jnp.int32, square, 1)
    owner_row = jnp.zeros(square, jnp.int32)
    owner_col = jnp.zeros((1, own_rows), jnp.int32)
    one_row = lax.broadcasted_iota(jnp.int32, (1, own_rows), 1)
    for r in range(per_group):
        owner_row = jnp.where(of_row // steps == r, homes[r], owner_row)
        owner_col = jnp.where(one_row // steps == r, homes[r], owner_col)
    owner_row, owner_col = owner_row // store_count, owner_col // store_count
    before = (owner_row == owner_col) & (of_row // steps < of_col // steps)
    placed = jnp.sum(before.astype(f32), axis=0, keepdims=True).astype(jnp.int32)
    want = owner_col * block + placed + lax.rem(one_row, steps)
    sent_row = lax.broadcasted_iota(jnp.int32, (sent_rows, own_rows), 0)
    pick_by_owner = (sent_row == want).astype(f32).astype(bf16)
    h_out = jnp.dot(pick_by_owner, hidden_rows, preferred_element_type=f32)
    h_send[...] = h_out.reshape(groups, block, width).astype(bf16)

    def copies(src, dst, ss, rs):
        out = []
        for j in range(groups - 1):
            d = step_to(j)
            out.append(
                pltpu.make_async_remote_copy(
                    src_ref=src(target(j)),
                    dst_ref=dst,
                    send_sem=ss.at[d - 1],
                    recv_sem=rs.at[d - 1],
                    device_id=send_to(j),
                    device_id_type=MESH,
                )
            )
        return out

    h_cp = copies(lambda t: h_send.at[t], h_all.at[me], h_ss, h_rs)

    for t in range(1, groups - 1):

        @pl.when(me < t)
        def _():
            pl.semaphore_wait(here.at[t], 1)

    @pl.when(upper == 0)
    def _():
        for c in h_cp[1:]:
            c.start()

    @pl.when(upper == 1)
    def _():
        for c in h_cp[:-1]:
            c.start()

    h_all[me] = h_send[me]

    lane = lax.broadcasted_iota(jnp.int32, (1, 128), 1)
    meta = jnp.zeros((1, 128), jnp.int32)
    for r in range(per_group):
        meta = jnp.where(lane == r, new_group[r], meta)
        meta = jnp.where(lane == per_group + r, cached_len[r], meta)
        owner = homes[r] // store_count
        pick = homes[r] - owner * store_count
        meta = jnp.where(lane == 2 * per_group + owner, pick, meta)
    meta_send[...] = meta
    m_cp = copies(lambda t: meta_send, meta_all.at[me], m_ss, m_rs)
    meta_all[me] = meta

    fetch[6].wait()
    sources = []
    for j in range(groups - 1):
        dest = target(j)
        count = jnp.int32(0)
        picked = [jnp.int32(0)] * move_cap
        for r in range(per_group):
            hit = new_group[r] == dest
            for k in range(move_cap):
                picked[k] = jnp.where(hit & (count == k), r, picked[k])
            count = count + hit.astype(jnp.int32)
        sources.append(picked)

    p_cp = {}

    def pack_pages(k, peers):
        for j in peers:
            slot = (step_to(j) - 1) * move_cap + k
            for i in range(pages):
                page_id = page_table[i, sources[j][k]]
                page_send[slot, :, pl.ds(i * page, page), :] = pool[:, page_id]
            for half in range(2):
                at = slice(None) if k < move_cap - 1 else half
                p_cp[j, k, half] = pltpu.make_async_remote_copy(
                    src_ref=page_send.at[slot, at],
                    dst_ref=rows.at[per_group + slot, at],
                    send_sem=p_ss.at[slot, half],
                    recv_sem=p_rs.at[slot, half],
                    device_id=send_to(j),
                    device_id_type=MESH,
                )
                if k < move_cap - 1:
                    break

    others = range(groups - 1)
    queue = [(j, 0) for j in others] + [(0, k) for k in range(1, move_cap)]
    queue += [(j, k) for k in range(1, move_cap) for j in others[:0:-1]]
    ahead = groups if move_cap > 1 else groups // 2

    def send_pages(some):
        for j, k in some:
            for half in range(1 if k < move_cap - 1 else 2):
                p_cp[j, k, half].start()

    first = [s for s in queue[:ahead] if s[1] == 0]
    straight = groups // 2 - 1
    pack_pages(0, [straight])
    send_pages([s for s in first if s[0] == straight])

    @pl.when(me < groups - 1)
    def _():
        pl.semaphore_wait(here.at[groups - 1], 1)

    @pl.when(upper == 0)
    def _():
        h_cp[0].start()

    @pl.when(upper == 1)
    def _():
        h_cp[-1].start()

    for c in m_cp:
        c.start()
    pack_pages(0, [j for j in others if j != straight])
    send_pages([s for s in first if s[0] != straight])

    @pl.when(me == 0)
    def _():
        pl.semaphore_wait(barrier, mps - 1)
        for device in beside:
            pl.semaphore_signal(columns, inc=1, device_id=device, device_id_type=MESH)
        pl.semaphore_wait(columns, mps - 1)
        for t in range(1, groups):
            pl.semaphore_signal(everyone, inc=1, device_id=(rep, t, mp), device_id_type=MESH)

    @pl.when(me > 0)
    def _():
        pl.semaphore_wait(everyone, 1)

    fetch[8].wait()
    for c in h_cp:
        c.wait_recv()
    h_in = h_all[...].astype(f32).reshape(sent_rows, width).astype(bf16)
    r_part[...] = lax.dot_general(
        h_in, a_panels[...], (((1,), (1,)), ((), ())), preferred_element_type=f32
    )
    r_cp = {}
    for d in range(1, mps):
        r_cp[d] = pltpu.make_async_remote_copy(
            src_ref=r_part,
            dst_ref=r_all.at[mp],
            send_sem=r_ss.at[d - 1],
            recv_sem=r_rs.at[d - 1],
            device_id=(rep, me, lax.rem(mp + d, mps)),
            device_id_type=MESH,
        )
        r_cp[d].start()
    r_all[mp] = r_part[...]

    for c in m_cp:
        c.wait_recv()
    local = pltpu.make_async_copy(meta_all, meta_s, l_sem)
    local.start()

    for k in range(1, move_cap):
        pack_pages(k, others)
    send_pages([s for s in queue[:ahead] if s[1] > 0])

    local.wait()
    mrow = lax.broadcasted_iota(jnp.int32, (sent_rows, lanes), 0) // block
    mlane = lax.broadcasted_iota(jnp.int32, (sent_rows, lanes), 1) // rank
    wanted = jnp.zeros((sent_rows, lanes), jnp.int32)
    for g in range(groups):
        wanted = jnp.where(mrow == g, meta_s[g, 0, 2 * per_group + me], wanted)

    fetch[9].wait()
    for d in range(1, mps):
        r_cp[d].wait_recv()
    total = r_all[0]
    for j in range(1, mps):
        total = total + r_all[j]
    total = jnp.where(mlane == wanted, total, 0.0).astype(bf16)
    delta = jnp.dot(total, b_panels[...], preferred_element_type=f32)
    d_send[...] = delta.reshape(groups, block, width).astype(bf16)
    d_cp = copies(lambda t: d_send.at[t], d_all.at[me], d_ss, d_rs)
    for c in d_cp:
        c.start()
    send_pages(queue[ahead:])
    d_all[me] = d_send[me]

    @pl.loop(0, per_group)
    def _(r):
        for j in range(pages):
            rows[r, :, pl.ds(j * page, page), :] = pool[:, page_table[j, r]]

    fetch[7].wait()
    fetch[10].wait()
    entry_slot = [jnp.int32(r) for r in range(per_group)]
    entry_len = [cached_len[r] for r in range(per_group)]
    source = [jnp.int32(r) for r in range(per_group)]
    for d in range(1, groups):
        origin = lax.rem(me + groups - d, groups)
        count = jnp.int32(0)
        slots = [jnp.int32(0)] * move_cap
        for r in range(per_group):
            hit = meta_s[origin, 0, r] == me
            for k in range(move_cap):
                slots[k] = jnp.where(hit & (count == k), r, slots[k])
            source[r] = jnp.where(
                hit,
                per_group + (d - 1) * move_cap + jnp.minimum(count, move_cap - 1),
                source[r],
            )
            count = count + hit.astype(jnp.int32)
        for k in range(move_cap):
            entry_slot.append(slots[k])
            entry_len.append(meta_s[origin, 0, per_group + slots[k]])
    near = sorted(range(1, groups), key=lambda d: min(d, groups - d))
    late = [per_group + (d - 1) * move_cap + move_cap - 1 for d in near]
    words = []
    for r in range(0, per_group, 4):
        words.append(sum(s << (8 * i) for i, s in enumerate(source[r : r + 4])))
    for e in late:
        real = functools.reduce(jnp.maximum, [(s == e).astype(jnp.int32) for s in source])
        words.append(entry_slot[e] * 2 + real)
    told_row = lax.broadcasted_iota(jnp.int32, info.shape, 0)
    told = jnp.zeros(info.shape, jnp.int32)
    for i, word in enumerate(words):
        told = jnp.where(told_row == i, word, told)
    info[...] = told

    ri = lax.broadcasted_iota(jnp.int32, (per_group * qr, per_kv * own_rows), 0)
    ci = lax.broadcasted_iota(jnp.int32, (per_group * qr, per_kv * own_rows), 1)
    place = (
        ci == (lax.rem(ri, qr) // steps) * own_rows + (ri // qr) * steps + lax.rem(ri, steps)
    )
    place = place.astype(f32).astype(bf16)
    base_rows = flat(frozen)

    for c in d_cp:
        c.wait_recv()
    d_in = d_all[...].astype(f32).reshape(sent_rows, width).astype(bf16)
    queries = base_rows + lax.dot_general(
        pick_by_owner, d_in, (((0,), (0,)), ((), ())), preferred_element_type=f32
    )
    for h in range(kv_heads):
        stack = jnp.concatenate(
            [
                queries[:, (h * per_kv + i) * HEAD : (h * per_kv + i + 1) * HEAD]
                for i in range(per_kv)
            ],
            axis=0,
        ).astype(bf16)
        got = jnp.dot(place, stack, preferred_element_type=f32)
        q_rows[:, h] = got.reshape(per_group, qr, HEAD).astype(bf16)

    def cols(h):
        return slice(h * HEAD, (h + 1) * HEAD)

    def scored(items):
        work = []
        for entry, slot, length in items:
            new = [fresh[slot, t].astype(f32) for t in range(steps)]
            for h in range(kv_heads):
                pairs = [(n[0:1, cols(h)], n[1:2, cols(h)]) for n in new]
                work.append((q_rows[slot, h], rows[entry, 0, :, cols(h)], length, pairs))
        return probabilities(work, steps, qr)

    def arrived(slot, at, half):
        pltpu.make_async_remote_copy(
            src_ref=page_send.at[slot, at],
            dst_ref=rows.at[per_group + slot, at],
            send_sem=p_ss.at[slot, half],
            recv_sem=p_rs.at[slot, half],
            device_id=send_to(0),
            device_id_type=MESH,
        ).wait_recv()

    def attend(items):
        prob, added = scored(items)
        for n, (entry, h) in enumerate((i[0], h) for i in items for h in range(kv_heads)):
            part = prob[n * qr : (n + 1) * qr]
            o = jnp.dot(part, rows[entry, 1, :, cols(h)], preferred_element_type=f32)
            att[entry, h] = (o + added[n]).astype(bf16)

    for r in range(0, per_group, 4):
        attend([(e, e, entry_len[e]) for e in range(r, min(r + 4, per_group))])
    for k in range(move_cap - 1):
        for n in range(0, len(near), 3):
            items = []
            for d in near[n : n + 3]:
                slot = (d - 1) * move_cap + k
                arrived(slot, slice(None), 0)
                e = per_group + slot
                items.append((e, entry_slot[e], entry_len[e]))
            attend(items)
    for e in late:
        att[e] = jnp.zeros(att.shape[1:], bf16)
    pr = lax.broadcasted_iota(jnp.int32, (per_kv * own_rows, per_group * qr), 0)
    pc = lax.broadcasted_iota(jnp.int32, (per_kv * own_rows, per_group * qr), 1)
    in_row = lax.rem(pr, own_rows)
    spread = (
        pc == (in_row // steps) * qr + (pr // own_rows) * steps + lax.rem(in_row, steps)
    )
    spread = spread.astype(f32).astype(bf16)
    for h in range(kv_heads):
        stack = jnp.concatenate([att[source[r], h] for r in range(per_group)], axis=0)
        got = jnp.dot(spread, stack, preferred_element_type=f32)
        for i in range(per_kv):
            wide[:, (h * per_kv + i) * HEAD : (h * per_kv + i + 1) * HEAD] = got[
                i * own_rows : (i + 1) * own_rows
            ]
    for r in range(per_group):
        early[r] = wide[r * steps : (r + 1) * steps].astype(bf16)

    for n in range(0, len(near), 3):
        batch = late[n : n + 3]
        for e in batch:
            arrived(e - per_group, 0, 0)
        prob, added = scored([(e, entry_slot[e], entry_len[e]) for e in batch])
        for i, (j, h) in enumerate((j, h) for j in range(len(batch)) for h in range(kv_heads)):
            prob_last[n + j, h] = prob[i * qr : (i + 1) * qr]
            new_last[n + j, h] = added[i]

    for c in h_cp + m_cp + d_cp:
        c.wait_send()
    for d in range(1, mps):
        r_cp[d].wait_send()
    for p in p_cp.values():
        p.wait_send()
    for e in late:
        arrived(e - per_group, 1, 1)


def finish(cfg, rows, early, info, prob_last, new_last, att_out, cache_out, late, c_sem, e_sem):
    groups, mps, per_group, steps, block, store_count, rank, pages, page, move_cap = cfg
    f32, bf16 = jnp.float32, jnp.bfloat16
    last, kv_heads, qr, _ = new_last.shape
    per_kv = qr // steps
    told = info[...]
    words = -(-per_group // 4)
    source = [(told[r // 4, 0] >> (8 * (r % 4))) & 255 for r in range(per_group)]
    out = [
        pltpu.make_async_copy(rows.at[source[r]], cache_out.at[:, r], c_sem.at[r])
        for r in range(per_group)
    ]
    for c in out:
        c.start()
    for r in range(per_group):
        from_last = (source[r] >= per_group) & (
            lax.rem(source[r] - per_group, move_cap) == move_cap - 1
        )

        @pl.when(jnp.logical_not(from_last))
        def _():
            pltpu.make_async_copy(early.at[r], att_out.at[r], e_sem.at[r]).start()

    near = sorted(range(1, groups), key=lambda d: min(d, groups - d))
    entry = [per_group + (d - 1) * move_cap + move_cap - 1 for d in near]
    for n in range(last):
        for h in range(kv_heads):
            values = rows[entry[n], 1, :, h * HEAD : (h + 1) * HEAD]
            o = new_last[n, h] + jnp.dot(prob_last[n, h], values, preferred_element_type=f32)
            for i in range(per_kv):
                late[n, :, (h * per_kv + i) * HEAD : (h * per_kv + i + 1) * HEAD] = o[
                    i * steps : (i + 1) * steps
                ].astype(bf16)
    for n in range(last):
        word = told[words + n, 0]
        slot = word // 2

        @pl.when(lax.rem(word, 2) == 1)
        def _():
            pltpu.make_async_copy(late.at[n], att_out.at[slot], e_sem.at[slot]).start()

    for r in range(per_group):
        out.append(pltpu.make_async_copy(early.at[r], att_out.at[r], e_sem.at[r]))
    for c in out:
        c.wait()


def per_device(
    hidden_in,
    frozen_query_rows,
    new_kv,
    adapter_of,
    adapter_home,
    a_store,
    b_store,
    kv_pool,
    page_table,
    cached_len,
    new_group,
):
    groups = lax.axis_size("req")
    mps = lax.axis_size("mp")
    per_group, steps, width = hidden_in.shape
    store_count, rank, _ = a_store.shape
    pages, page = page_table.shape[1], kv_pool.shape[2]
    kv_width = kv_pool.shape[3]
    context = pages * page
    move_cap = -(-(per_group - per_group // 4) // groups)
    cap = -(-per_group // min(16, groups))
    block = -(-cap * steps // 8) * 8
    lanes = store_count * rank
    qr = width // kv_width * steps
    kv_heads = kv_width // HEAD
    moved = (groups - 1) * move_cap
    last = groups - 1
    entries = per_group + moved
    bf16, f32, i32 = jnp.bfloat16, jnp.float32, jnp.int32
    cfg = (groups, mps, per_group, steps, block, store_count, rank, pages, page, move_cap)
    dma = pltpu.SemaphoreType.DMA
    given = (
        adapter_of,
        adapter_home,
        page_table.T,
        cached_len,
        new_group,
        hidden_in,
        kv_pool,
        frozen_query_rows,
        a_store.reshape(lanes, width),
        b_store.reshape(lanes, width),
        new_kv,
    )
    passed = (
        jax.ShapeDtypeStruct((entries, 2, context, kv_width), bf16),
        jax.ShapeDtypeStruct((per_group, steps, width), bf16),
        jax.ShapeDtypeStruct((-(-(-(-per_group // 4) + last) // 8) * 8, 128), i32),
        jax.ShapeDtypeStruct((last, kv_heads, qr, context), bf16),
        jax.ShapeDtypeStruct((last, kv_heads, qr, HEAD), f32),
    )
    scratch = [
        VMEM((groups, block, width), bf16),
        VMEM((groups, block, width), bf16),
        VMEM((groups * block, lanes), f32),
        VMEM((mps, groups * block, lanes), f32),
        VMEM((groups, block, width), bf16),
        VMEM((groups, block, width), bf16),
        VMEM((per_group, kv_heads, qr, HEAD), bf16),
        VMEM((per_group * steps, width), f32),
        VMEM((1, 128), i32),
        VMEM((groups, 1, 128), i32),
        SMEM((groups, 1, 128), i32),
        VMEM((moved, 2, context, kv_width), bf16),
        VMEM((entries, kv_heads, qr, HEAD), bf16),
        dma((groups - 1,)),
        dma((groups - 1,)),
        dma((mps - 1,)),
        dma((mps - 1,)),
        dma((groups - 1,)),
        dma((groups - 1,)),
        dma((groups - 1,)),
        dma((groups - 1,)),
        dma((moved, 2)),
        dma((moved, 2)),
        dma,
        pltpu.SemaphoreType.REGULAR((groups,)),
        pltpu.SemaphoreType.REGULAR,
        pltpu.SemaphoreType.REGULAR,
    ]

    def first(*refs):
        n = len(given)
        held = n + len(passed)
        exchange(
            cfg, refs[:n], refs[n:held], refs[held : held + n], refs[held + n], *refs[held + n + 1 :]
        )

    between = pl.pallas_call(
        first,
        out_shape=passed,
        in_specs=[pl.BlockSpec(memory_space=HBM)] * len(given),
        out_specs=[pl.BlockSpec(memory_space=VMEM)] * len(passed),
        scratch_shapes=[SMEM(g.shape, g.dtype) for g in given[:5]]
        + [VMEM(g.shape, g.dtype) for g in given[5:]]
        + [dma((len(given),))]
        + scratch,
        compiler_params=pltpu.CompilerParams(
            collective_id=0, has_side_effects=True, vmem_limit_bytes=32 * 2**20
        ),
        name="exchange",
    )(*[pltpu.with_memory_space_constraint(g, HBM) for g in given])
    return pl.pallas_call(
        functools.partial(finish, cfg),
        out_shape=(
            jax.ShapeDtypeStruct((per_group, steps, width), bf16),
            jax.ShapeDtypeStruct((2, per_group, context, kv_width), bf16),
        ),
        in_specs=[
            pl.BlockSpec(memory_space=m) for m in (VMEM, VMEM, VMEM, VMEM, VMEM)
        ],
        out_specs=[pl.BlockSpec(memory_space=HBM)] * 2,
        scratch_shapes=[
            VMEM((last, steps, width), bf16),
            dma((per_group,)),
            dma((per_group,)),
        ],
        compiler_params=pltpu.CompilerParams(vmem_limit_bytes=16 * 2**20),
        name="finish",
    )(*between)


def solution(mesh):
    placed = (
        P(("rep", "req"), None, "mp"),
        P(("rep", "req"), None, "mp"),
        P(("rep", "req"), None, None, "mp"),
        P(("rep", "req")),
        P("rep"),
        P(("rep", "req"), None, "mp"),
        P(("rep", "req"), None, "mp"),
        P(None, ("rep", "req"), None, "mp"),
        P(("rep", "req"), None),
        P(("rep", "req")),
        P(("rep", "req")),
    )
    return jax.shard_map(
        per_device,
        mesh=mesh,
        in_specs=placed,
        out_specs=(P(("rep", "req"), None, "mp"), P(None, ("rep", "req"), None, "mp")),
        check_vma=False,
    )
```
